128 devices in a mesh: grp: 4 (over z_hi, core), ep: 32 (over y, x, z_lo).
Axes of the slice: x: 4, y: 4, z: 4 (z_hi: 2, z_lo: 2; z = z_hi * 2 + z_lo), core: 2. Of those that a mesh axis runs over, the one named last changes fastest.
Arguments:
- hidden: bfloat16 [16384, 8, 768], P(('grp', 'ep')), may hold values from -1.5 to 1.5
- out_grad: bfloat16 [16384, 4096], P(('grp', 'ep')), may hold values from -6 to 6
- route_ids: int32 [16384, 8], P(('grp', 'ep')), may hold values from 0 to 127, all different within a row; in each aligned block of 128 rows (0 to 127, 128 to 255, ...) at most 12 rows name the same one
- gate_vals: float32 [16384, 8], P(('grp', 'ep')), may hold values from 0.05 to 0.5
- rollout_ids: int32 [128, 128], P(('grp', 'ep')), may hold values from 0 to 3, never falling along the last dimension, each value on 1 to 64 neighbouring positions
- advantages: float32 [128, 4], P(('grp', 'ep')), may hold values from -3 to 3
- down_weight: bfloat16 [128, 768, 4096], P(('grp', 'ep')), may hold values from -0.09375 to 0.09375
Outputs:
- hidden_grad: bfloat16 [16384, 8, 768], P(('grp', 'ep'))
- weight_grad: bfloat16 [128, 768, 4096], P(('grp', 'ep'))
The draws below stay inside these ranges and needn't reach their ends.
Inputs may be any that keep to these rules, and one draw needn't show every extreme that they name: `route_ids`: each row names 8 different experts; among the 128 rows of one device no expert is named more than 12 times, a bound that some block reaches there. `rollout_ids`: within each row the ids never fall; every id 0 to 3 appears, at most 128 // 2 times.
All inputs are finite; a program needn't handle non-finite values.
Results may differ from the reference program's by a relative error of at most 0.0049.
Values may be sent and summed in bfloat16 or wider, within the bound.
A program may use at most 192 MiB of HBM per device.

```python
import math
import jax
import jax.numpy as jnp
import numpy as np
from jax import lax

D = 4096
FF = 768
TOPK = 8
TOK_DEV = 128
ROLL_DEV = 4
EXPERTS = 128
TOKENS = 16384
CAP = 12
DEVICES = 128


def steps_of(own_key, shape, split, smallest, top_value):
    def one(dim, parts):
        steps = jax.random.uniform(jax.random.fold_in(jax.random.fold_in(own_key, 6), dim), (parts,), jnp.float32, smallest / len(split), top_value / len(split))
        return jnp.repeat(jnp.exp(steps), shape[dim] // parts).reshape((-1,) + (1,) * (len(shape) - dim - 1))

    level = one(*split[0])
    for cut in split[1:]:
        level = level * one(*cut)
    return level


def split_up(count, total, most, slope):
    loads = [(1 << 20) // math.isqrt(grade ** slope) + 1 for grade in range(2, count + 1)]
    surplus, given = total - most - (count - 1), [1] * (count - 1)
    while surplus > 0:
        movable = [i for i in range(count - 1) if given[i] < most]
        pool, budget = sum([loads[i] for i in movable]), surplus
        for i in movable:
            extra = min(most - given[i], max(1, budget * loads[i] // pool), surplus)
            given[i] = given[i] + extra
            surplus = surplus - extra
    return np.array([most] + given)


def uneven(key, amount, total, limit, skew):
    if amount == 2:
        one = jax.random.randint(key, (), max(1, total - limit), min(limit, total - 1) + 1)
        return jnp.stack([one, total - one])
    lengths = jnp.asarray(split_up(amount, total, limit, skew), jnp.int32)
    twos = (amount - 1) // 2
    giver, taker = lengths[1:1 + 2 * twos:2], lengths[2:2 + 2 * twos:2]
    slack = jnp.minimum(giver - 1, limit - taker)
    shifted = jax.random.randint(jax.random.fold_in(key, 1), (twos,), 0, 1 << 20) % (slack + 1)
    lengths = lengths.at[1:1 + 2 * twos:2].set(giver - shifted).at[2:2 + 2 * twos:2].set(taker + shifted)
    return lengths[jax.random.permutation(jax.random.fold_in(key, 2), amount)]


def shared_out(stream_key, own, number, rows, count, top, limit, lean):
    order = jax.random.permutation(stream_key, count)
    crowded, common = load_shares(count, rows * top, limit, lean, True), load_shares(count, rows * top, limit, lean, False)
    places = jnp.arange(count)

    def named(tallies, turn):
        used = int((tallies > 0).sum())
        fixed = max(1, used // 4)
        shifted = fixed + (places - fixed + turn * (used - fixed)) % max(1, count - fixed)
        return jnp.zeros((count,), jnp.int32).at[order[jnp.where(places < fixed, places, shifted)]].set(jnp.asarray(tallies, jnp.int32))

    tallies = jnp.where(number % 4 == 0, named(crowded, number // 4), named(common, number - number // 4 - 1))
    mixed = jax.random.permutation(jax.random.fold_in(own, 3), count)
    source_of, taker = mixed[0:count // 2 * 2:2], mixed[1:count // 2 * 2:2]
    slack = jnp.minimum(tallies[source_of] - 1, limit - tallies[taker]) // 2
    slack = jnp.where((source_of == order[0]) | (taker == order[0]) | (tallies[taker] == 0), 0, jnp.maximum(slack, 0))
    shifted = jax.random.randint(jax.random.fold_in(own, 4), (count // 2,), 0, 1 << 20) % (slack + 1)
    tallies = tallies.at[source_of].add(-shifted).at[taker].add(shifted)
    items = jnp.searchsorted(jnp.cumsum(tallies), jnp.arange(rows * top), side="right").astype(jnp.int32)
    table = items.reshape(top, rows).T
    table = table[jax.random.permutation(jax.random.fold_in(own, 1), rows)]
    turn = jax.random.randint(jax.random.fold_in(own, 2), (rows, 1), 0, top)
    return jnp.take_along_axis(table, (jnp.arange(top)[None, :] + turn) % top, axis=1)


def load_shares(number_of, total, limit, skew, full):
    loads = [(1 << 20) // math.isqrt(standing ** skew) + 1 for standing in range(1, number_of + 1)]
    largest = limit if full else min(limit, max(-(-total // number_of), total * loads[0] // sum(loads)))
    least = 1 if total - largest >= number_of - 1 else 0
    given, spare = [largest] + [least] * (number_of - 1), total - largest - least * (number_of - 1)
    while spare > 0:
        candidates = [i for i in range(1, number_of) if given[i] < largest] or [i for i in range(1, number_of) if given[i] < limit]
        pool, budget = sum([loads[i] for i in candidates]), spare
        for i in candidates:
            extra = min(limit - given[i], max(1, budget * loads[i] // pool), spare)
            given[i] = given[i] + extra
            spare = spare - extra
    return np.array(given)


def gaussian(rng, extent, scale, most, pieces=(), held_as=jnp.bfloat16):
    entries = jax.random.normal(rng, extent, jnp.float32) * scale
    if len(pieces) > 0:
        entries = steps_of(rng, extent, pieces, -0.22, 0.18) * entries
    return jnp.clip(entries, min=-most, max=most).astype(held_as)


def setup_inputs(seed: int = 0) -> dict:
    streams_of = jax.random.split(jax.random.key(seed), 8)
    hidden = gaussian(streams_of[0], (TOKENS, TOPK, FF), 0.25, 1.5, ((0, 128),))
    out_grad = gaussian(streams_of[1], (TOKENS, D), 1.0, 6.0, ((0, 128),))
    route_ids_keys = jax.random.split(jax.random.fold_in(streams_of[2], 1), TOKENS // TOK_DEV)
    route_ids_turns = jax.random.permutation(jax.random.fold_in(streams_of[2], 3), TOKENS // TOK_DEV)
    route_ids = jax.vmap(lambda own, number: shared_out(jax.random.fold_in(streams_of[2], 2), own, number, TOK_DEV, EXPERTS, TOPK, CAP, 2))(route_ids_keys, route_ids_turns).reshape((TOKENS, TOPK))
    gate_vals = jnp.clip(jnp.exp(math.log(0.5) - 2.3025851 * jax.random.uniform(streams_of[3], (TOKENS, TOPK), jnp.float32) ** steps_of(streams_of[3], (TOKENS, TOPK), ((0, 128),), -0.2, 0.2)), 0.05, 0.5)
    rollout_ids = jax.vmap(lambda own: jnp.searchsorted(jnp.cumsum(uneven(own, ROLL_DEV, TOK_DEV, TOK_DEV // 2, 1)), jnp.arange(TOK_DEV), side="right"))(jax.random.split(streams_of[4], DEVICES)).reshape((DEVICES, TOK_DEV)).astype(jnp.int32)
    advantages = gaussian(streams_of[5], (DEVICES, ROLL_DEV), 1.0, 3.0, ((0, 128),), jnp.float32)
    down_weight = gaussian(streams_of[6], (EXPERTS, FF, D), D ** -0.5, 0.09375, ((0, 128),))
    return dict(hidden=hidden, out_grad=out_grad, route_ids=route_ids, gate_vals=gate_vals, rollout_ids=rollout_ids, advantages=advantages, down_weight=down_weight)


def reference(hidden, out_grad, route_ids, gate_vals, rollout_ids, advantages, down_weight):
    rows_all = DEVICES * CAP
    slots_all = TOKENS * TOPK
    member = (rollout_ids[:, :, None] == jnp.arange(ROLL_DEV, dtype=jnp.int32)[None, None, :]).astype(jnp.float32)
    counts = jnp.sum(member, axis=1)
    roll_weight = advantages * (TOK_DEV / ROLL_DEV) / counts
    token_weight = jnp.sum(member * roll_weight[:, None, :], axis=2).reshape(TOKENS)
    slot_scale = (gate_vals * token_weight[:, None]).reshape(slots_all)
    flat_ids = route_ids.reshape(DEVICES, TOK_DEV * TOPK).astype(jnp.int32)
    one_hot = (flat_ids[:, :, None] == jnp.arange(EXPERTS, dtype=jnp.int32)[None, None, :]).astype(jnp.int32)
    before = jnp.cumsum(one_hot, axis=1) - one_hot
    slot_rank = jnp.sum(before * one_hot, axis=2).astype(jnp.int32)
    device_base = (jnp.arange(DEVICES, dtype=jnp.int32) * CAP)[:, None]
    position = (flat_ids * rows_all + device_base + slot_rank).reshape(slots_all)
    source = jnp.full((EXPERTS * rows_all,), slots_all, jnp.int32)
    source = source.at[position].set(jnp.arange(slots_all, dtype=jnp.int32)).reshape(EXPERTS, rows_all)
    hidden_pad = jnp.concatenate([hidden.reshape(slots_all, FF), jnp.zeros((1, FF), jnp.bfloat16)], axis=0)
    grad_pad = jnp.concatenate([out_grad, jnp.zeros((1, D), jnp.bfloat16)], axis=0)
    scale_pad = jnp.concatenate([slot_scale, jnp.zeros((1,), jnp.float32)], axis=0)

    def expert_work(pair):
        weight, picks = pair
        hidden_rows = hidden_pad[picks]
        token_index = jnp.where(picks < slots_all, picks // TOPK, TOKENS).astype(jnp.int32)
        scaled_rows = (scale_pad[picks][:, None] * grad_pad[token_index].astype(jnp.float32)).astype(jnp.bfloat16)
        weight_grad = lax.dot_general(hidden_rows, scaled_rows, (((0,), (0,)), ((), ())), preferred_element_type=jnp.float32)
        returned = lax.dot_general(scaled_rows, weight, (((1,), (1,)), ((), ())), preferred_element_type=jnp.float32)
        return weight_grad.astype(jnp.bfloat16), returned.astype(jnp.bfloat16)

    weight_grad, returned = lax.map(expert_work, (down_weight, source))
    hidden_grad = returned.reshape(EXPERTS * rows_all, FF)[position].reshape(TOKENS, TOPK, FF)
    return hidden_grad, weight_grad
```

```python
import functools

import jax
import jax.numpy as jnp
from jax import lax
from jax.experimental import pallas as pl
from jax.experimental.pallas import tpu as pltpu
from jax.sharding import PartitionSpec as P

MESH = pl.DeviceIdType.MESH
SIDE = 4
CAP = 12
PICK = SIDE * CAP
WIDTHS = (1408, 1408, 1280)
STARTS = (0, 1408, 2816)


def position():
    group, owner = lax.axis_index("grp"), lax.axis_index("ep")
    core = group % 2
    z = (group // 2) * 2 + owner % 2
    x = (owner // 2) % 4
    y = owner // 8
    return (x, y, z), core


def place(coords, core):
    x, y, z = coords
    return ((z // 2) * 2 + core, y * 8 + x * 2 + z % 2)


def moved(coords, axis, by):
    new = list(coords)
    new[axis] = (coords[axis] + by) % SIDE
    return tuple(new)


def expert_rows(part):
    row = lax.broadcasted_iota(jnp.int32, (128, 128), 0)
    coords = [None] * 3
    coords[part % 3] = row // 32
    coords[(part + 1) % 3] = (row // 8) % 4
    coords[(part + 2) % 3] = (row // 2) % 4
    x, y, z = coords
    return ((z // 2) * 2 + row % 2) * 32 + y * 8 + x * 2 + z % 2


def dispatch_kernel(
    route_ref,
    gate_ref,
    rollout_ref,
    adv_ref,
    grad_ref,
    out0,
    out1,
    out2,
    lines0,
    lines1,
    lines2,
    tables,
    got_tables,
    picks,
    send0,
    send1,
    send2,
    mid0,
    mid1,
    mid2,
    local_sem,
    line_send,
    line_recv,
    table_send,
    table_recv,
    mid_send,
    mid_recv,
    last_send,
    last_recv,
):
    outs, lines = (out0, out1, out2), (lines0, lines1, lines2)
    sends, mids = (send0, send1, send2), (mid0, mid1, mid2)
    here, core = position()

    barrier = pltpu.get_barrier_semaphore()
    for axis in range(3):
        for by in range(SIDE):
            for flip in range(2):
                if (by or flip) and (by or axis == 0):
                    pl.semaphore_signal(
                        barrier,
                        inc=1,
                        device_id=place(moved(here, axis, by), (core + flip) % 2),
                        device_id_type=MESH,
                    )
    pl.semaphore_wait(barrier, 19)

    def line_copy(part, by):
        there = place(moved(here, part, by), core)
        return pltpu.make_async_remote_copy(
            src_ref=grad_ref.at[:, pl.ds(STARTS[part], WIDTHS[part])],
            dst_ref=lines[part].at[pl.ds(pl.multiple_of(here[part] * 128, 128), 128)],
            send_sem=line_send.at[part, by],
            recv_sem=line_recv.at[part, by],
            device_id=there,
            device_id_type=MESH,
        )

    def own_line(part):
        return pltpu.make_async_copy(
            grad_ref.at[:, pl.ds(STARTS[part], WIDTHS[part])],
            lines[part].at[pl.ds(pl.multiple_of(here[part] * 128, 128), 128)],
            local_sem.at[part],
        )

    def table_copy(part, by):
        target = moved(here, part, by)
        return pltpu.make_async_remote_copy(
            src_ref=tables.at[part, target[part]],
            dst_ref=got_tables.at[part, here[part]],
            send_sem=table_send.at[part, by],
            recv_sem=table_recv.at[part, by],
            device_id=place(target, core),
            device_id_type=MESH,
        )

    def own_table(part):
        return pltpu.make_async_copy(
            tables.at[part, here[part]], got_tables.at[part, here[part]], local_sem.at[3 + part]
        )

    for by in (1, 3, 2):
        for part in range(3):
            line_copy(part, by).start()
    for part in range(3):
        own_line(part).start()

    rollout = rollout_ref[...]
    weight = jnp.zeros((1, 128), jnp.float32)
    for i in range(4):
        hit = (rollout == i).astype(jnp.float32)
        count = jnp.sum(hit, axis=1, keepdims=True)
        weight = weight + hit * (adv_ref[:, i : i + 1] * 32.0 / count)
    scale = gate_ref[...] * weight
    route = route_ref[...]
    sooner = (
        lax.broadcasted_iota(jnp.int32, (128, 128), 0)
        < lax.broadcasted_iota(jnp.int32, (128, 128), 1)
    ).astype(jnp.bfloat16)
    for part in range(3):
        expert = expert_rows(part)
        named = jnp.zeros((128, 128), jnp.float32)
        held = jnp.zeros((128, 128), jnp.float32)
        for k in range(8):
            match = route[k : k + 1, :] == expert
            named = named + jnp.where(match, 1.0, 0.0)
            held = held + jnp.where(match, scale[k : k + 1, :], 0.0)
        rank = jnp.dot(named.astype(jnp.bfloat16), sooner, preferred_element_type=jnp.float32)
        rank = jnp.where(named > 0.5, rank, -1.0)
        for i in range(SIDE):
            tables[part, i, 0:32] = rank[32 * i : 32 * i + 32]
            tables[part, i, 32:64] = held[32 * i : 32 * i + 32]
    for by in (1, 3, 2):
        for part in range(3):
            table_copy(part, by).start()
    for part in range(3):
        own_table(part).start()

    def mid_copy(part, by):
        return pltpu.make_async_remote_copy(
            src_ref=sends[part].at[by],
            dst_ref=mids[part].at[by - 1],
            send_sem=mid_send.at[part, by],
            recv_sem=mid_recv.at[part, by],
            device_id=place(moved(here, (part + 1) % 3, by), core),
            device_id_type=MESH,
        )

    def last_copy(part, by, step, flip, source):
        second, third = (part + 1) % 3, (part + 2) % 3
        target = moved(here, third, step)
        there_core = (core + flip) % 2
        rows = pl.ds(pl.multiple_of((target[third] * 2 + there_core) * PICK, PICK), PICK)
        origin = (here[second] + SIDE - by) % SIDE
        block = (here[third] * 2 + core) * SIDE + origin
        return source.at[rows], outs[part].at[block], target, there_core

    def last_remote(part, by, index, source):
        step, flip = index // 2, index % 2
        src, dst, target, there_core = last_copy(part, by, step, flip, source)
        return pltpu.make_async_remote_copy(
            src_ref=src,
            dst_ref=dst,
            send_sem=last_send.at[part, by, index],
            recv_sem=last_recv.at[part, by, index],
            device_id=place(target, there_core),
            device_id_type=MESH,
        )

    def last_local(part, by, source):
        src, dst, _, _ = last_copy(part, by, 0, 0, source)
        return pltpu.make_async_copy(src, dst, last_recv.at[part, by, 0])

    def forward(part, by, source):
        last_local(part, by, source).start()

        def body(index, carry):
            last_remote(part, by, index, source).start()
            return carry

        lax.fori_loop(1, 8, body, 0)

    row = lax.broadcasted_iota(jnp.int32, (PICK, 512), 0)
    lane = lax.broadcasted_iota(jnp.int32, (PICK, 512), 1)
    wanted = jnp.where(lane // 128 == row // CAP, row % CAP, -7).astype(jnp.float32)

    for part in range(3):
        own_line(part).wait()
        own_table(part).wait()
        for by in (1, 3, 2):
            line_copy(part, by).wait()
            table_copy(part, by).wait()

    for part in range(3):

        def select(i, carry, part=part):
            by = (i + 1) % SIDE
            target = (here[(part + 1) % 3] + by) % SIDE
            first = pl.multiple_of(target * 8, 8)
            ranks = jnp.concatenate(
                [got_tables[part, s, pl.ds(first, 8), :] for s in range(SIDE)], axis=1
            )
            helds = jnp.concatenate(
                [got_tables[part, s, pl.ds(first + 32, 8), :] for s in range(SIDE)], axis=1
            )
            scales = []
            for j in range(8):
                hit = ranks[j : j + 1, :] == wanted
                picks[pl.ds(j * PICK, PICK), :] = jnp.where(hit, 1.0, 0.0).astype(jnp.bfloat16)
                scales.append(
                    jnp.sum(jnp.where(hit, helds[j : j + 1, :], 0.0), axis=1, keepdims=True)
                )
            factor = jnp.concatenate(scales, axis=0)
            for start in range(0, WIDTHS[part], 256):
                width = min(256, WIDTHS[part] - start)
                found = jnp.dot(
                    picks[...],
                    lines[part][:, start : start + width],
                    preferred_element_type=jnp.float32,
                )
                sends[part][by, :, start : start + width] = (found * factor).astype(jnp.bfloat16)

            @pl.when(by > 0)
            def _():
                mid_copy(part, by).start()

            return carry

        lax.fori_loop(0, SIDE, select, 0)
        forward(part, 0, sends[part].at[0])

    for by in (1, 2, 3):
        for part in range(3):
            mid_copy(part, by).wait()
            forward(part, by, mids[part].at[by - 1])

    for part in range(3):

        def finish(i, carry, part=part):
            last_local(part, i, sends[part].at[0]).wait()

            def body(index, inner):
                last_remote(part, i, index, sends[part].at[0]).wait()
                return inner

            return lax.fori_loop(1, 8, body, carry)

        lax.fori_loop(0, SIDE, finish, 0)


def dispatch(route_t, gate_t, rollout_ids, advantages, out_grad):
    vmem = pl.BlockSpec(memory_space=pltpu.VMEM)
    scratch = [pltpu.VMEM((512, w), jnp.bfloat16) for w in WIDTHS]
    scratch += [
        pltpu.VMEM((3, SIDE, 64, 128), jnp.float32),
        pltpu.VMEM((3, SIDE, 64, 128), jnp.float32),
        pltpu.VMEM((8 * PICK, 512), jnp.bfloat16),
    ]
    scratch += [pltpu.VMEM((SIDE, 8 * PICK, w), jnp.bfloat16) for w in WIDTHS]
    scratch += [pltpu.VMEM((SIDE - 1, 8 * PICK, w), jnp.bfloat16) for w in WIDTHS]
    scratch += [pltpu.SemaphoreType.DMA((6,))]
    scratch += [pltpu.SemaphoreType.DMA((3, SIDE)) for _ in range(6)]
    scratch += [pltpu.SemaphoreType.DMA((3, SIDE, 8)) for _ in range(2)]
    return pl.pallas_call(
        dispatch_kernel,
        out_shape=[jax.ShapeDtypeStruct((32, PICK, w), jnp.bfloat16) for w in WIDTHS],
        in_specs=[vmem] * 5,
        out_specs=[pl.BlockSpec(memory_space=pl.ANY)] * 3,
        scratch_shapes=scratch,
        compiler_params=pltpu.CompilerParams(
            collective_id=0, has_side_effects=True, vmem_limit_bytes=50 << 20
        ),
    )(route_t, gate_t, rollout_ids, advantages, out_grad)


def ordered(rows, part):
    width = rows.shape[-1]
    names = ("zh", "c", "y", "x", "zl")
    grid = rows.reshape(2, 2, 4, 4, 2, CAP, width)
    at = {n: i for i, n in enumerate(names)}
    axes = {"x": ["x"], "y": ["y"], "z": ["zh", "zl"]}
    order = "xyz"
    first, second, third = (order[(part + i) % 3] for i in range(3))
    want = axes[third] + ["c"] + axes[second] + axes[first]
    return grid.transpose([at[n] for n in want] + [5, 6]).reshape(1536, width)


def unordered(rows, part):
    width = rows.shape[-1]
    names = ["zh", "c", "y", "x", "zl"]
    size = {"zh": 2, "c": 2, "y": 4, "x": 4, "zl": 2}
    axes = {"x": ["x"], "y": ["y"], "z": ["zh", "zl"]}
    order = "xyz"
    first, second, third = (order[(part + i) % 3] for i in range(3))
    have = axes[third] + ["c"] + axes[second] + axes[first]
    grid = rows.reshape([size[n] for n in have] + [CAP, width])
    return grid.transpose([have.index(n) for n in names] + [5, 6]).reshape(1536, width)


def shards(hidden, out_grad, route_ids, gate_vals, rollout_ids, advantages, down_weight):
    slots = 1024
    flat_ids = route_ids.reshape(slots)
    named = jnp.sum(
        (route_ids[:, :, None] == jnp.arange(128, dtype=jnp.int32)).astype(jnp.bfloat16), axis=1
    )
    t = jnp.arange(128, dtype=jnp.int32)
    earlier = (t[:, None] > t[None, :]).astype(jnp.bfloat16)
    before = jnp.dot(earlier, named, preferred_element_type=jnp.float32)
    rank = jnp.sum(
        jnp.where(
            route_ids[:, :, None] == jnp.arange(128, dtype=jnp.int32), before[:, None, :], 0.0
        ),
        axis=2,
    ).astype(jnp.int32)
    spot = (route_ids * CAP + rank).reshape(slots)
    one_hot = (jnp.arange(1536, dtype=jnp.int32)[:, None] == spot[None, :]).astype(jnp.bfloat16)

    parts = dispatch(route_ids.T, gate_vals.T, rollout_ids, advantages, out_grad)
    hidden_send = jnp.dot(
        one_hot, hidden.reshape(slots, 768), preferred_element_type=jnp.float32
    ).astype(jnp.bfloat16)

    def exchange(rows):
        rows = rows.reshape(128, 24, 384)
        rows = lax.all_to_all(rows, ("grp", "ep"), split_axis=0, concat_axis=0, tiled=True)
        return rows.reshape(1536, 768)

    got_hidden = exchange(hidden_send)
    weight = down_weight[0]
    grads = []
    answers = jnp.zeros((1536, 768), jnp.float32)
    for part in range(3):
        got = parts[part].reshape(1536, WIDTHS[part])
        grads.append(
            lax.dot_general(
                ordered(got_hidden, part),
                got,
                (((0,), (0,)), ((), ())),
                preferred_element_type=jnp.float32,
            ).astype(jnp.bfloat16)
        )
        answer = lax.dot_general(
            got,
            weight[:, STARTS[part] : STARTS[part] + WIDTHS[part]],
            (((1,), (1,)), ((), ())),
            preferred_element_type=jnp.float32,
        )
        answers = answers + unordered(answer, part)
    weight_grad = jnp.concatenate(grads, axis=1)
    returned = exchange(answers.astype(jnp.bfloat16))
    hidden_grad = lax.dot_general(
        one_hot, returned, (((0,), (0,)), ((), ())), preferred_element_type=jnp.float32
    ).astype(jnp.bfloat16)
    return hidden_grad.reshape(128, 8, 768), weight_grad[None]


def solution(mesh):
    wide = P(("grp", "ep"), None, None)
    flat = P(("grp", "ep"), None)
    return jax.shard_map(
        shards,
        mesh=mesh,
        in_specs=(wide, flat, flat, flat, flat, flat, wide),
        out_specs=(wide, wide),
        check_vma=False,
    )
```

```python
import functools

import jax
import jax.numpy as jnp
from jax import lax
from jax.experimental import pallas as pl
from jax.experimental.pallas import tpu as pltpu
from jax.sharding import PartitionSpec as P

MESH = pl.DeviceIdType.MESH
SIDE = 4
CAP = 12
PICK = SIDE * CAP
WIDTHS = (1280, 1280, 1536)
STARTS = (0, 1280, 2560)


def position():
    group, owner = lax.axis_index("grp"), lax.axis_index("ep")
    core = group % 2
    z = (group // 2) * 2 + owner % 2
    x = (owner // 2) % 4
    y = owner // 8
    return (x, y, z), core


def place(coords, core):
    x, y, z = coords
    return ((z // 2) * 2 + core, y * 8 + x * 2 + z % 2)


def moved(coords, axis, by):
    new = list(coords)
    new[axis] = (coords[axis] + by) % SIDE
    return tuple(new)


def expert_rows(part):
    row = lax.broadcasted_iota(jnp.int32, (128, 128), 0)
    coords = [None] * 3
    coords[part % 3] = row // 32
    coords[(part + 1) % 3] = (row // 8) % 4
    coords[(part + 2) % 3] = (row // 2) % 4
    x, y, z = coords
    return ((z // 2) * 2 + row % 2) * 32 + y * 8 + x * 2 + z % 2


def dispatch_kernel(
    route_ref,
    gate_ref,
    rollout_ref,
    adv_ref,
    grad_ref,
    weight_ref,
    kept0,
    kept1,
    kept2,
    answer_ref,
    weight,
    total,
    answer,
    out0,
    out1,
    out2,
    lines0,
    lines1,
    lines2,
    tables,
    got_tables,
    picks,
    send0,
    send1,
    send2,
    mid0,
    mid1,
    mid2,
    local_sem,
    keep_sem,
    line_send,
    line_recv,
    table_send,
    table_recv,
    mid_send,
    mid_recv,
    last_send,
    last_recv,
):
    outs, lines = (out0, out1, out2), (lines0, lines1, lines2)
    kept = (kept0, kept1, kept2)
    sends, mids = (send0, send1, send2), (mid0, mid1, mid2)
    here, core = position()

    barrier = pltpu.get_barrier_semaphore()
    for axis in range(3):
        for by in range(SIDE):
            for flip in range(2):
                if (by or flip) and (by or axis == 0):
                    pl.semaphore_signal(
                        barrier,
                        inc=1,
                        device_id=place(moved(here, axis, by), (core + flip) % 2),
                        device_id_type=MESH,
                    )
    pl.semaphore_wait(barrier, 19)

    def line_copy(part, by):
        there = place(moved(here, part, by), core)
        return pltpu.make_async_remote_copy(
            src_ref=grad_ref.at[:, pl.ds(STARTS[part], WIDTHS[part])],
            dst_ref=lines[part].at[pl.ds(pl.multiple_of(here[part] * 128, 128), 128)],
            send_sem=line_send.at[part, by],
            recv_sem=line_recv.at[part, by],
            device_id=there,
            device_id_type=MESH,
        )

    def own_line(part):
        return pltpu.make_async_copy(
            grad_ref.at[:, pl.ds(STARTS[part], WIDTHS[part])],
            lines[part].at[pl.ds(pl.multiple_of(here[part] * 128, 128), 128)],
            local_sem.at[part],
        )

    def table_copy(part, by):
        target = moved(here, part, by)
        return pltpu.make_async_remote_copy(
            src_ref=tables.at[part, target[part]],
            dst_ref=got_tables.at[part, here[part]],
            send_sem=table_send.at[part, by],
            recv_sem=table_recv.at[part, by],
            device_id=place(target, core),
            device_id_type=MESH,
        )

    def own_table(part):
        return pltpu.make_async_copy(
            tables.at[part, here[part]], got_tables.at[part, here[part]], local_sem.at[3 + part]
        )

    for by in (1, 3, 2):
        for part in range(3):
            line_copy(part, by).start()
    for part in range(3):
        own_line(part).start()
    load_weight = pltpu.make_async_copy(weight_ref.at[0], weight, local_sem.at[6])
    load_weight.start()

    rollout = rollout_ref[...]
    token_weight = jnp.zeros((1, 128), jnp.float32)
    for i in range(4):
        hit = (rollout == i).astype(jnp.float32)
        count = jnp.sum(hit, axis=1, keepdims=True)
        token_weight = token_weight + hit * (adv_ref[:, i : i + 1] * 32.0 / count)
    scale = gate_ref[...] * token_weight
    route = route_ref[...]
    sooner = (
        lax.broadcasted_iota(jnp.int32, (128, 128), 0)
        < lax.broadcasted_iota(jnp.int32, (128, 128), 1)
    ).astype(jnp.bfloat16)
    for part in range(3):
        expert = expert_rows(part)
        named = jnp.zeros((128, 128), jnp.float32)
        held = jnp.zeros((128, 128), jnp.float32)
        for k in range(8):
            match = route[k : k + 1, :] == expert
            named = named + jnp.where(match, 1.0, 0.0)
            held = held + jnp.where(match, scale[k : k + 1, :], 0.0)
        rank = jnp.dot(named.astype(jnp.bfloat16), sooner, preferred_element_type=jnp.float32)
        rank = jnp.where(named > 0.5, rank, -1.0)
        for i in range(SIDE):
            tables[part, i, 0:32] = rank[32 * i : 32 * i + 32]
            tables[part, i, 32:64] = held[32 * i : 32 * i + 32]
    for by in (1, 3, 2):
        for part in range(3):
            table_copy(part, by).start()
    for part in range(3):
        own_table(part).start()

    def mid_copy(part, by):
        return pltpu.make_async_remote_copy(
            src_ref=sends[part].at[by],
            dst_ref=mids[part].at[by - 1],
            send_sem=mid_send.at[part, by],
            recv_sem=mid_recv.at[part, by],
            device_id=place(moved(here, (part + 1) % 3, by), core),
            device_id_type=MESH,
        )

    def last_copy(part, by, step, flip, source):
        second, third = (part + 1) % 3, (part + 2) % 3
        target = moved(here, third, step)
        there_core = (core + flip) % 2
        rows = pl.ds(pl.multiple_of((target[third] * 2 + there_core) * PICK, PICK), PICK)
        origin = (here[second] + SIDE - by) % SIDE
        block = here[third] * 2 + core
        return source.at[rows], outs[part].at[block, origin], target, there_core

    def last_remote(part, by, index, source):
        step, flip = index // 2, index % 2
        src, dst, target, there_core = last_copy(part, by, step, flip, source)
        return pltpu.make_async_remote_copy(
            src_ref=src,
            dst_ref=dst,
            send_sem=last_send.at[part, by, index],
            recv_sem=last_recv.at[part, by, index],
            device_id=place(target, there_core),
            device_id_type=MESH,
        )

    def last_local(part, by, source):
        src, dst, _, _ = last_copy(part, by, 0, 0, source)
        return pltpu.make_async_copy(src, dst, last_recv.at[part, by, 0])

    def forward(part, by, source):
        last_local(part, by, source).start()

        def body(index, carry):
            last_remote(part, by, index, source).start()
            return carry

        lax.fori_loop(1, 8, body, 0)

    row = lax.broadcasted_iota(jnp.int32, (PICK, 512), 0)
    lane = lax.broadcasted_iota(jnp.int32, (PICK, 512), 1)
    wanted = jnp.where(lane // 128 == row // CAP, row % CAP, -7).astype(jnp.float32)

    for part in range(3):
        own_line(part).wait()
        own_table(part).wait()
        for by in (1, 3, 2):
            line_copy(part, by).wait()
            table_copy(part, by).wait()

    for part in range(3):

        def select(i, carry, part=part):
            by = (i + 1) % SIDE
            target = (here[(part + 1) % 3] + by) % SIDE
            first = pl.multiple_of(target * 8, 8)
            ranks = jnp.concatenate(
                [got_tables[part, s, pl.ds(first, 8), :] for s in range(SIDE)], axis=1
            )
            helds = jnp.concatenate(
                [got_tables[part, s, pl.ds(first + 32, 8), :] for s in range(SIDE)], axis=1
            )
            scales = []
            for j in range(8):
                hit = ranks[j : j + 1, :] == wanted
                picks[pl.ds(j * PICK, PICK), :] = jnp.where(hit, 1.0, 0.0).astype(jnp.bfloat16)
                scales.append(
                    jnp.sum(jnp.where(hit, helds[j : j + 1, :], 0.0), axis=1, keepdims=True)
                )
            factor = jnp.concatenate(scales, axis=0)
            for start in range(0, WIDTHS[part], 256):
                width = min(256, WIDTHS[part] - start)
                found = jnp.dot(
                    picks[...],
                    lines[part][:, start : start + width],
                    preferred_element_type=jnp.float32,
                )
                sends[part][by, :, start : start + width] = (found * factor).astype(jnp.bfloat16)

            @pl.when(by > 0)
            def _():
                mid_copy(part, by).start()

            return carry

        lax.fori_loop(0, SIDE, select, 0)
        forward(part, 0, sends[part].at[0])

    def keep(part, by):
        origin = (here[(part + 1) % 3] + SIDE - by) % SIDE
        return pltpu.make_async_copy(
            outs[part].at[:, origin], kept[part].at[:, origin], keep_sem.at[part, by]
        )

    def absorb(part, by):
        last_local(part, by, mids[part].at[0]).wait()

        def arrive(index, carry):
            last_remote(part, by, index, mids[part].at[0]).wait_recv()
            return carry

        lax.fori_loop(1, 8, arrive, 0)
        keep(part, by).start()
        origin = (here[(part + 1) % 3] + SIDE - by) % SIDE
        rows = outs[part][:, origin].reshape(8 * PICK, WIDTHS[part])
        product = lax.dot_general(
            rows,
            weight[:, STARTS[part] : STARTS[part] + WIDTHS[part]],
            (((1,), (1,)), ((), ())),
            preferred_element_type=jnp.float32,
        )
        for block in range(8):
            for j in range(SIDE):
                coords = [None] * 3
                coords[part] = j
                coords[(part + 1) % 3] = origin
                coords[(part + 2) % 3] = block // 2
                group, owner = place(coords, block % 2)
                first = block * PICK + j * CAP
                device = group * 32 + owner
                total[device] = total[device] + product[first : first + CAP]

    total[...] = jnp.zeros_like(total)
    load_weight.wait()

    def onward(step, carry):
        @pl.when(step < SIDE)
        def _():
            for part in range(3):
                mid_copy(part, step).wait()
                forward(part, step, mids[part].at[step - 1])

        for part in range(3):
            absorb(part, step - 1)
        return carry

    lax.fori_loop(1, SIDE + 1, onward, 0)

    def pack(device, carry):
        rows = total[device]
        rows = jnp.concatenate([rows[:, :384], rows[:, 384:]], axis=0)
        answer[device] = rows.astype(jnp.bfloat16)
        return carry

    lax.fori_loop(0, 128, pack, 0)
    give = pltpu.make_async_copy(answer, answer_ref, local_sem.at[7])
    give.start()

    for part in range(3):

        def finish(i, carry, part=part):
            keep(part, i).wait()

            def body(index, inner):
                last_remote(part, i, index, mids[part].at[0]).wait_send()
                return inner

            return lax.fori_loop(1, 8, body, carry)

        lax.fori_loop(0, SIDE, finish, 0)
    give.wait()


def dispatch(route_t, gate_t, rollout_ids, advantages, out_grad, down_weight):
    vmem = pl.BlockSpec(memory_space=pltpu.VMEM)
    hbm = pl.BlockSpec(memory_space=pl.ANY)
    scratch = [
        pltpu.VMEM((768, 4096), jnp.bfloat16),
        pltpu.VMEM((128, CAP, 768), jnp.float32),
        pltpu.VMEM((128, 2 * CAP, 384), jnp.bfloat16),
    ]
    scratch += [pltpu.VMEM((8, SIDE, PICK, w), jnp.bfloat16) for w in WIDTHS]
    scratch += [pltpu.VMEM((512, w), jnp.bfloat16) for w in WIDTHS]
    scratch += [
        pltpu.VMEM((3, SIDE, 64, 128), jnp.float32),
        pltpu.VMEM((3, SIDE, 64, 128), jnp.float32),
        pltpu.VMEM((8 * PICK, 512), jnp.bfloat16),
    ]
    scratch += [pltpu.VMEM((SIDE, 8 * PICK, w), jnp.bfloat16) for w in WIDTHS]
    scratch += [pltpu.VMEM((SIDE - 1, 8 * PICK, w), jnp.bfloat16) for w in WIDTHS]
    scratch += [pltpu.SemaphoreType.DMA((8,))]
    scratch += [pltpu.SemaphoreType.DMA((3, SIDE)) for _ in range(7)]
    scratch += [pltpu.SemaphoreType.DMA((3, SIDE, 8)) for _ in range(2)]
    shapes = [jax.ShapeDtypeStruct((8, SIDE, PICK, w), jnp.bfloat16) for w in WIDTHS]
    shapes += [jax.ShapeDtypeStruct((128, 2 * CAP, 384), jnp.bfloat16)]
    return pl.pallas_call(
        dispatch_kernel,
        out_shape=shapes,
        in_specs=[vmem] * 5 + [hbm],
        out_specs=[hbm] * 4,
        scratch_shapes=scratch,
        compiler_params=pltpu.CompilerParams(
            collective_id=0, has_side_effects=True, vmem_limit_bytes=62 << 20
        ),
    )(route_t, gate_t, rollout_ids, advantages, out_grad, down_weight)


def arrange_kernel(got_ref, *out_refs):
    for part in range(3):

        def block_of(block, carry, part=part):
            pieces = []
            for j in range(SIDE):
                coords = [None] * 3
                coords[part] = j
                coords[(part + 1) % 3] = block % SIDE
                coords[(part + 2) % 3] = block // 8
                group, owner = place(coords, (block // SIDE) % 2)
                rows = got_ref[group * 32 + owner].astype(jnp.float32)
                pieces.append(jnp.concatenate([rows[:CAP], rows[CAP:]], axis=1))
            first = pl.multiple_of(block * PICK, PICK)
            out_refs[part][pl.ds(first, PICK)] = jnp.concatenate(pieces, axis=0).astype(
                jnp.bfloat16
            )
            return carry

        lax.fori_loop(0, 32, block_of, 0)


def arrange(got):
    vmem = pl.BlockSpec(memory_space=pltpu.VMEM)
    return pl.pallas_call(
        arrange_kernel,
        out_shape=[jax.ShapeDtypeStruct((1536, 768), jnp.bfloat16)] * 3,
        in_specs=[vmem],
        out_specs=[vmem] * 3,
        compiler_params=pltpu.CompilerParams(vmem_limit_bytes=24 << 20),
        cost_estimate=pl.CostEstimate(flops=0, bytes_accessed=10 << 20, transcendentals=0),
    )(got)


def shards(hidden, out_grad, route_ids, gate_vals, rollout_ids, advantages, down_weight):
    slots = 1024
    flat_ids = route_ids.reshape(slots)
    named = jnp.sum(
        (route_ids[:, :, None] == jnp.arange(128, dtype=jnp.int32)).astype(jnp.bfloat16), axis=1
    )
    t = jnp.arange(128, dtype=jnp.int32)
    earlier = (t[:, None] > t[None, :]).astype(jnp.bfloat16)
    before = jnp.dot(earlier, named, preferred_element_type=jnp.float32)
    rank = jnp.sum(
        jnp.where(
            route_ids[:, :, None] == jnp.arange(128, dtype=jnp.int32), before[:, None, :], 0.0
        ),
        axis=2,
    ).astype(jnp.int32)
    spot = (route_ids * CAP + rank).reshape(slots)
    one_hot = (jnp.arange(1536, dtype=jnp.int32)[:, None] == spot[None, :]).astype(jnp.bfloat16)

    parts = dispatch(
        route_ids.T, gate_vals.T, rollout_ids, advantages, out_grad, down_weight
    )
    hidden_send = jnp.dot(
        one_hot, hidden.reshape(slots, 768), preferred_element_type=jnp.float32
    ).astype(jnp.bfloat16)

    def exchange(rows):
        return lax.all_to_all(rows, ("grp", "ep"), split_axis=0, concat_axis=0, tiled=True)

    got_hidden = exchange(
        hidden_send.reshape(128, CAP, 2, 384).transpose(0, 2, 1, 3).reshape(128, 2 * CAP, 384)
    )
    returned = exchange(parts[3])
    grads = [
        lax.dot_general(
            rows,
            part.reshape(1536, width),
            (((0,), (0,)), ((), ())),
            preferred_element_type=jnp.float32,
        ).astype(jnp.bfloat16)
        for rows, part, width in zip(arrange(got_hidden), parts[:3], WIDTHS)
    ]
    weight_grad = jnp.concatenate(grads, axis=1)
    returned = returned.reshape(128, 2, CAP, 384).transpose(0, 2, 1, 3).reshape(1536, 768)
    hidden_grad = lax.dot_general(
        one_hot, returned, (((0,), (0,)), ((), ())), preferred_element_type=jnp.float32
    ).astype(jnp.bfloat16)
    return hidden_grad.reshape(128, 8, 768), weight_grad[None]


def solution(mesh):
    wide = P(("grp", "ep"), None, None)
    flat = P(("grp", "ep"), None)
    return jax.shard_map(
        shards,
        mesh=mesh,
        in_specs=(wide, flat, flat, flat, flat, flat, wide),
        out_specs=(wide, wide),
        check_vma=False,
    )
```

```python
import functools

import jax
import jax.numpy as jnp
from jax import lax
from jax.experimental import pallas as pl
from jax.experimental.pallas import tpu as pltpu
from jax.sharding import PartitionSpec as P

MESH = pl.DeviceIdType.MESH
SIDE = 4
CAP = 12
STRIDE = 77
PICK = SIDE * CAP
WIDTHS = (1280, 1280, 1536)
STARTS = (0, 1280, 2560)


def position():
    group, owner = lax.axis_index("grp"), lax.axis_index("ep")
    core = group % 2
    z = (group // 2) * 2 + owner % 2
    x = (owner // 2) % 4
    y = owner // 8
    return (x, y, z), core


def place(coords, core):
    x, y, z = coords
    return ((z // 2) * 2 + core, y * 8 + x * 2 + z % 2)


def moved(coords, axis, by):
    new = list(coords)
    new[axis] = (coords[axis] + by) % SIDE
    return tuple(new)


def expert_rows(part):
    row = lax.broadcasted_iota(jnp.int32, (128, 128), 0)
    coords = [None] * 3
    coords[part % 3] = row // 32
    coords[(part + 1) % 3] = (row // 8) % 4
    coords[(part + 2) % 3] = (row // 2) % 4
    x, y, z = coords
    return ((z // 2) * 2 + row % 2) * 32 + y * 8 + x * 2 + z % 2


def dispatch_kernel(
    route_ref,
    gate_ref,
    rollout_ref,
    adv_ref,
    grad_ref,
    spot_ref,
    hidden_ref,
    weight_ref,
    kept0,
    kept1,
    kept2,
    answer_ref,
    got_hidden,
    weight,
    total,
    answer,
    out0,
    out1,
    out2,
    lines0,
    lines1,
    lines2,
    tables,
    got_tables,
    picks,
    send0,
    send1,
    send2,
    mid0,
    mid1,
    mid2,
    local_sem,
    keep_sem,
    line_send,
    line_recv,
    table_send,
    table_recv,
    mid_send,
    mid_recv,
    last_send,
    last_recv,
    hidden_send,
    hidden_recv,
):
    outs, lines = (out0, out1, out2), (lines0, lines1, lines2)
    kept = (kept0, kept1, kept2)
    sends, mids = (send0, send1, send2), (mid0, mid1, mid2)
    here, core = position()

    barrier = pltpu.get_barrier_semaphore()
    me = lax.axis_index("grp") * 32 + lax.axis_index("ep")

    def other(index):
        shift = (index * STRIDE) % 128
        x, y, z = here
        coords = ((x + shift // 2) % SIDE, (y + shift // 8) % SIDE, (z + shift // 32) % SIDE)
        return place(coords, (core + shift) % 2)

    def greet(index, carry):
        pl.semaphore_signal(barrier, inc=1, device_id=other(index), device_id_type=MESH)
        return carry

    lax.fori_loop(1, 128, greet, 0)
    pl.semaphore_wait(barrier, 127)

    def line_copy(part, by):
        there = place(moved(here, part, by), core)
        return pltpu.make_async_remote_copy(
            src_ref=grad_ref.at[:, pl.ds(STARTS[part], WIDTHS[part])],
            dst_ref=lines[part].at[pl.ds(pl.multiple_of(here[part] * 128, 128), 128)],
            send_sem=line_send.at[part, by],
            recv_sem=line_recv.at[part, by],
            device_id=there,
            device_id_type=MESH,
        )

    def own_line(part):
        return pltpu.make_async_copy(
            grad_ref.at[:, pl.ds(STARTS[part], WIDTHS[part])],
            lines[part].at[pl.ds(pl.multiple_of(here[part] * 128, 128), 128)],
            local_sem.at[part],
        )

    def table_copy(part, by):
        target = moved(here, part, by)
        return pltpu.make_async_remote_copy(
            src_ref=tables.at[part, target[part]],
            dst_ref=got_tables.at[part, here[part]],
            send_sem=table_send.at[part, by],
            recv_sem=table_recv.at[part, by],
            device_id=place(target, core),
            device_id_type=MESH,
        )

    def own_table(part):
        return pltpu.make_async_copy(
            tables.at[part, here[part]], got_tables.at[part, here[part]], local_sem.at[3 + part]
        )

    for by in (1, 3, 2):
        for part in range(3):
            line_copy(part, by).start()
    for part in range(3):
        own_line(part).start()
    load_weight = pltpu.make_async_copy(weight_ref.at[0], weight, local_sem.at[6])
    load_weight.start()

    rollout = rollout_ref[...]
    token_weight = jnp.zeros((1, 128), jnp.float32)
    for i in range(4):
        hit = (rollout == i).astype(jnp.float32)
        count = jnp.sum(hit, axis=1, keepdims=True)
        token_weight = token_weight + hit * (adv_ref[:, i : i + 1] * 32.0 / count)
    scale = gate_ref[...] * token_weight
    route = route_ref[...]
    sooner = (
        lax.broadcasted_iota(jnp.int32, (128, 128), 0)
        < lax.broadcasted_iota(jnp.int32, (128, 128), 1)
    ).astype(jnp.bfloat16)
    for part in range(3):
        expert = expert_rows(part)
        named = jnp.zeros((128, 128), jnp.float32)
        held = jnp.zeros((128, 128), jnp.float32)
        for k in range(8):
            match = route[k : k + 1, :] == expert
            named = named + jnp.where(match, 1.0, 0.0)
            held = held + jnp.where(match, scale[k : k + 1, :], 0.0)
        rank = jnp.dot(named.astype(jnp.bfloat16), sooner, preferred_element_type=jnp.float32)
        rank = jnp.where(named > 0.5, rank, -1.0)
        for i in range(SIDE):
            tables[part, i, 0:32] = rank[32 * i : 32 * i + 32]
            tables[part, i, 32:64] = held[32 * i : 32 * i + 32]
    for by in (1, 3, 2):
        for part in range(3):
            table_copy(part, by).start()
    for part in range(3):
        own_table(part).start()

    def hidden_copy(index):
        group, owner = other(index)
        return pltpu.make_async_remote_copy(
            src_ref=answer.at[group * 32 + owner],
            dst_ref=got_hidden.at[me],
            send_sem=hidden_send.at[index],
            recv_sem=hidden_recv.at[index],
            device_id=(group, owner),
            device_id_type=MESH,
        )

    own_hidden = pltpu.make_async_copy(answer.at[me], got_hidden.at[me], local_sem.at[8])

    def gather(block, carry):
        wanted_spot = lax.broadcasted_iota(jnp.int32, (384, 1024), 0) + block * 384
        pick = jnp.where(wanted_spot == spot_ref[...], 1.0, 0.0).astype(jnp.bfloat16)
        found = jnp.dot(pick, hidden_ref[...], preferred_element_type=jnp.float32)
        for i in range(32):
            rows = found[i * CAP : i * CAP + CAP]
            rows = jnp.concatenate([rows[:, :384], rows[:, 384:]], axis=0)
            answer[block * 32 + i] = rows.astype(jnp.bfloat16)
        return carry

    lax.fori_loop(0, 4, gather, 0)
    own_hidden.start()

    def mid_copy(part, by):
        return pltpu.make_async_remote_copy(
            src_ref=sends[part].at[by],
            dst_ref=mids[part].at[by - 1],
            send_sem=mid_send.at[part, by],
            recv_sem=mid_recv.at[part, by],
            device_id=place(moved(here, (part + 1) % 3, by), core),
            device_id_type=MESH,
        )

    def last_copy(part, by, step, flip, source):
        second, third = (part + 1) % 3, (part + 2) % 3
        target = moved(here, third, step)
        there_core = (core + flip) % 2
        rows = pl.ds(pl.multiple_of((target[third] * 2 + there_core) * PICK, PICK), PICK)
        origin = (here[second] + SIDE - by) % SIDE
        block = here[third] * 2 + core
        return source.at[rows], outs[part].at[block, origin], target, there_core

    def last_remote(part, by, index, source):
        step, flip = index // 2, index % 2
        src, dst, target, there_core = last_copy(part, by, step, flip, source)
        return pltpu.make_async_remote_copy(
            src_ref=src,
            dst_ref=dst,
            send_sem=last_send.at[part, by, index],
            recv_sem=last_recv.at[part, by, index],
            device_id=place(target, there_core),
            device_id_type=MESH,
        )

    def last_local(part, by, source):
        src, dst, _, _ = last_copy(part, by, 0, 0, source)
        return pltpu.make_async_copy(src, dst, last_recv.at[part, by, 0])

    def forward(part, by, source):
        last_local(part, by, source).start()

        def body(index, carry):
            last_remote(part, by, index, source).start()
            return carry

        lax.fori_loop(1, 8, body, 0)

    row = lax.broadcasted_iota(jnp.int32, (PICK, 512), 0)
    lane = lax.broadcasted_iota(jnp.int32, (PICK, 512), 1)
    wanted = jnp.where(lane // 128 == row // CAP, row % CAP, -7).astype(jnp.float32)

    for part in range(3):
        own_line(part).wait()
        own_table(part).wait()
        for by in (1, 3, 2):
            line_copy(part, by).wait()
            table_copy(part, by).wait()

    for part in range(3):

        def select(i, carry, part=part):
            by = (i + 1) % SIDE
            target = (here[(part + 1) % 3] + by) % SIDE
            first = pl.multiple_of(target * 8, 8)
            ranks = jnp.concatenate(
                [got_tables[part, s, pl.ds(first, 8), :] for s in range(SIDE)], axis=1
            )
            helds = jnp.concatenate(
                [got_tables[part, s, pl.ds(first + 32, 8), :] for s in range(SIDE)], axis=1
            )
            scales = []
            for j in range(8):
                hit = ranks[j : j + 1, :] == wanted
                picks[pl.ds(j * PICK, PICK), :] = jnp.where(hit, 1.0, 0.0).astype(jnp.bfloat16)
                scales.append(
                    jnp.sum(jnp.where(hit, helds[j : j + 1, :], 0.0), axis=1, keepdims=True)
                )
            factor = jnp.concatenate(scales, axis=0)
            for start in range(0, WIDTHS[part], 256):
                width = min(256, WIDTHS[part] - start)
                found = jnp.dot(
                    picks[...],
                    lines[part][:, start : start + width],
                    preferred_element_type=jnp.float32,
                )
                sends[part][by, :, start : start + width] = (found * factor).astype(jnp.bfloat16)

            @pl.when(by > 0)
            def _():
                mid_copy(part, by).start()

            return carry

        lax.fori_loop(0, SIDE, select, 0)
        forward(part, 0, sends[part].at[0])

    def keep(part, by):
        origin = (here[(part + 1) % 3] + SIDE - by) % SIDE
        return pltpu.make_async_copy(
            outs[part].at[:, origin], kept[part].at[:, origin], keep_sem.at[part, by]
        )

    def absorb(part, by):
        last_local(part, by, mids[part].at[0]).wait()

        def arrive(index, carry):
            last_remote(part, by, index, mids[part].at[0]).wait_recv()
            return carry

        lax.fori_loop(1, 8, arrive, 0)
        keep(part, by).start()
        origin = (here[(part + 1) % 3] + SIDE - by) % SIDE
        rows = outs[part][:, origin].reshape(8 * PICK, WIDTHS[part])
        product = lax.dot_general(
            rows,
            weight[:, STARTS[part] : STARTS[part] + WIDTHS[part]],
            (((1,), (1,)), ((), ())),
            preferred_element_type=jnp.float32,
        )
        for block in range(8):
            for j in range(SIDE):
                coords = [None] * 3
                coords[part] = j
                coords[(part + 1) % 3] = origin
                coords[(part + 2) % 3] = block // 2
                group, owner = place(coords, block % 2)
                first = block * PICK + j * CAP
                device = group * 32 + owner
                total[device] = total[device] + product[first : first + CAP]

    total[...] = jnp.zeros_like(total)
    load_weight.wait()

    def push(index, carry):
        hidden_copy(index).start()
        return carry

    def onward(step, carry):
        @pl.when(step < SIDE)
        def _():
            for part in range(3):
                mid_copy(part, step).wait()
                forward(part, step, mids[part].at[step - 1])

        @pl.when(step < SIDE - 1)
        def _():
            lax.fori_loop(64 * step - 63, jnp.minimum(64 * step + 1, 128), push, 0)

        for part in range(3):
            absorb(part, step - 1)
        return carry

    lax.fori_loop(1, SIDE + 1, onward, 0)

    def settle(index, carry):
        hidden_copy(index).wait_send()
        return carry

    def collect(index, carry):
        hidden_copy(index).wait_recv()
        return carry

    own_hidden.wait()
    lax.fori_loop(1, 128, settle, 0)

    def pack(device, carry):
        rows = total[device]
        rows = jnp.concatenate([rows[:, :384], rows[:, 384:]], axis=0)
        answer[device] = rows.astype(jnp.bfloat16)
        return carry

    lax.fori_loop(0, 128, pack, 0)
    give = pltpu.make_async_copy(answer, answer_ref, local_sem.at[7])
    give.start()

    for part in range(3):

        def finish(i, carry, part=part):
            keep(part, i).wait()

            def body(index, inner):
                last_remote(part, i, index, mids[part].at[0]).wait_send()
                return inner

            return lax.fori_loop(1, 8, body, carry)

        lax.fori_loop(0, SIDE, finish, 0)
    lax.fori_loop(1, 128, collect, 0)
    give.wait()


def dispatch(*operands):
    vmem = pl.BlockSpec(memory_space=pltpu.VMEM)
    hbm = pl.BlockSpec(memory_space=pl.ANY)
    scratch = [
        pltpu.VMEM((768, 4096), jnp.bfloat16),
        pltpu.VMEM((128, CAP, 768), jnp.float32),
        pltpu.VMEM((128, 2 * CAP, 384), jnp.bfloat16),
    ]
    scratch += [pltpu.VMEM((8, SIDE, PICK, w), jnp.bfloat16) for w in WIDTHS]
    scratch += [pltpu.VMEM((512, w), jnp.bfloat16) for w in WIDTHS]
    scratch += [
        pltpu.VMEM((3, SIDE, 64, 128), jnp.float32),
        pltpu.VMEM((3, SIDE, 64, 128), jnp.float32),
        pltpu.VMEM((8 * PICK, 512), jnp.bfloat16),
    ]
    scratch += [pltpu.VMEM((SIDE, 8 * PICK, w), jnp.bfloat16) for w in WIDTHS]
    scratch += [pltpu.VMEM((SIDE - 1, 8 * PICK, w), jnp.bfloat16) for w in WIDTHS]
    scratch += [pltpu.SemaphoreType.DMA((9,))]
    scratch += [pltpu.SemaphoreType.DMA((3, SIDE)) for _ in range(7)]
    scratch += [pltpu.SemaphoreType.DMA((3, SIDE, 8)) for _ in range(2)]
    scratch += [pltpu.SemaphoreType.DMA((128,)) for _ in range(2)]
    shapes = [jax.ShapeDtypeStruct((8, SIDE, PICK, w), jnp.bfloat16) for w in WIDTHS]
    shapes += [jax.ShapeDtypeStruct((128, 2 * CAP, 384), jnp.bfloat16)] * 2
    return pl.pallas_call(
        dispatch_kernel,
        out_shape=shapes,
        in_specs=[vmem] * 7 + [hbm],
        out_specs=[hbm] * 5,
        scratch_shapes=scratch,
        compiler_params=pltpu.CompilerParams(
            collective_id=0, has_side_effects=True, vmem_limit_bytes=62 << 20
        ),
    )(*operands)


def arrange_kernel(got_ref, *out_refs):
    for part in range(3):

        def block_of(block, carry, part=part):
            pieces = []
            for j in range(SIDE):
                coords = [None] * 3
                coords[part] = j
                coords[(part + 1) % 3] = block % SIDE
                coords[(part + 2) % 3] = block // 8
                group, owner = place(coords, (block // SIDE) % 2)
                rows = got_ref[group * 32 + owner].astype(jnp.float32)
                pieces.append(jnp.concatenate([rows[:CAP], rows[CAP:]], axis=1))
            first = pl.multiple_of(block * PICK, PICK)
            out_refs[part][pl.ds(first, PICK)] = jnp.concatenate(pieces, axis=0).astype(
                jnp.bfloat16
            )
            return carry

        lax.fori_loop(0, 32, block_of, 0)


def arrange(got):
    vmem = pl.BlockSpec(memory_space=pltpu.VMEM)
    return pl.pallas_call(
        arrange_kernel,
        out_shape=[jax.ShapeDtypeStruct((1536, 768), jnp.bfloat16)] * 3,
        in_specs=[vmem],
        out_specs=[vmem] * 3,
        compiler_params=pltpu.CompilerParams(vmem_limit_bytes=24 << 20),
        cost_estimate=pl.CostEstimate(flops=0, bytes_accessed=10 << 20, transcendentals=0),
    )(got)


def shards(hidden, out_grad, route_ids, gate_vals, rollout_ids, advantages, down_weight):
    slots = 1024
    flat_ids = route_ids.reshape(slots)
    named = jnp.sum(
        (route_ids[:, :, None] == jnp.arange(128, dtype=jnp.int32)).astype(jnp.bfloat16), axis=1
    )
    t = jnp.arange(128, dtype=jnp.int32)
    earlier = (t[:, None] > t[None, :]).astype(jnp.bfloat16)
    before = jnp.dot(earlier, named, preferred_element_type=jnp.float32)
    rank = jnp.sum(
        jnp.where(
            route_ids[:, :, None] == jnp.arange(128, dtype=jnp.int32), before[:, None, :], 0.0
        ),
        axis=2,
    ).astype(jnp.int32)
    spot = (route_ids * CAP + rank).reshape(slots)
    one_hot = (jnp.arange(1536, dtype=jnp.int32)[:, None] == spot[None, :]).astype(jnp.bfloat16)

    parts = dispatch(
        route_ids.T,
        gate_vals.T,
        rollout_ids,
        advantages,
        out_grad,
        spot[None, :],
        hidden.reshape(slots, 768),
        down_weight,
    )

    def exchange(rows):
        return lax.all_to_all(rows, ("grp", "ep"), split_axis=0, concat_axis=0, tiled=True)

    got_hidden = parts[4]
    returned = exchange(parts[3])
    grads = [
        lax.dot_general(
            rows,
            part.reshape(1536, width),
            (((0,), (0,)), ((), ())),
            preferred_element_type=jnp.float32,
        ).astype(jnp.bfloat16)
        for rows, part, width in zip(arrange(got_hidden), parts[:3], WIDTHS)
    ]
    weight_grad = jnp.concatenate(grads, axis=1)
    returned = returned.reshape(128, 2, CAP, 384).transpose(0, 2, 1, 3).reshape(1536, 768)
    hidden_grad = lax.dot_general(
        one_hot, returned, (((0,), (0,)), ((), ())), preferred_element_type=jnp.float32
    ).astype(jnp.bfloat16)
    return hidden_grad.reshape(128, 8, 768), weight_grad[None]


def solution(mesh):
    wide = P(("grp", "ep"), None, None)
    flat = P(("grp", "ep"), None)
    return jax.shard_map(
        shards,
        mesh=mesh,
        in_specs=(wide, flat, flat, flat, flat, flat, wide),
        out_specs=(wide, wide),
        check_vma=False,
    )
```

```python
import jax
import jax.numpy as jnp
from jax import lax
from jax.experimental import pallas as pl
from jax.experimental.pallas import tpu as pltpu
from jax.sharding import PartitionSpec as P

MESH = pl.DeviceIdType.MESH
SIDE = 4
CAP = 12
STRIDE = 77
PICK = SIDE * CAP
WIDTHS = (1280, 1280, 1536)
STARTS = (0, 1280, 2560)


def position():
    group, owner = lax.axis_index("grp"), lax.axis_index("ep")
    core = group % 2
    z = (group // 2) * 2 + owner % 2
    x = (owner // 2) % 4
    y = owner // 8
    return (x, y, z), core


def place(coords, core):
    x, y, z = coords
    return ((z // 2) * 2 + core, y * 8 + x * 2 + z % 2)


def moved(coords, axis, by):
    new = list(coords)
    new[axis] = (coords[axis] + by) % SIDE
    return tuple(new)


def expert_rows(part):
    row = lax.broadcasted_iota(jnp.int32, (128, 128), 0)
    coords = [None] * 3
    coords[part % 3] = row // 32
    coords[(part + 1) % 3] = (row // 8) % 4
    coords[(part + 2) % 3] = (row // 2) % 4
    x, y, z = coords
    return ((z // 2) * 2 + row % 2) * 32 + y * 8 + x * 2 + z % 2


def dispatch_kernel(
    route_ref,
    gate_ref,
    rollout_ref,
    adv_ref,
    grad_ref,
    spot_ref,
    hidden_ref,
    weight_ref,
    kept0,
    kept1,
    kept2,
    answer_ref,
    got_hidden,
    weight,
    total,
    answer,
    out0,
    out1,
    out2,
    lines0,
    lines1,
    lines2,
    tables,
    got_tables,
    picks,
    send0,
    send1,
    send2,
    mid0,
    mid1,
    mid2,
    local_sem,
    keep_sem,
    line_send,
    line_recv,
    table_send,
    table_recv,
    mid_send,
    mid_recv,
    last_send,
    last_recv,
    hidden_send,
    hidden_recv,
):
    outs, lines = (out0, out1, out2), (lines0, lines1, lines2)
    kept = (kept0, kept1, kept2)
    sends, mids = (send0, send1, send2), (mid0, mid1, mid2)
    here, core = position()

    barrier = pltpu.get_barrier_semaphore()
    me = lax.axis_index("grp") * 32 + lax.axis_index("ep")

    def other(index):
        shift = (index * STRIDE) % 128
        x, y, z = here
        coords = ((x + shift // 2) % SIDE, (y + shift // 8) % SIDE, (z + shift // 32) % SIDE)
        return place(coords, (core + shift) % 2)

    def greet(index, carry):
        pl.semaphore_signal(barrier, inc=1, device_id=other(index), device_id_type=MESH)
        return carry

    lax.fori_loop(1, 128, greet, 0)
    pl.semaphore_wait(barrier, 127)

    def line_copy(part, by):
        there = place(moved(here, part, by), core)
        return pltpu.make_async_remote_copy(
            src_ref=grad_ref.at[:, pl.ds(STARTS[part], WIDTHS[part])],
            dst_ref=lines[part].at[pl.ds(pl.multiple_of(here[part] * 128, 128), 128)],
            send_sem=line_send.at[part, by],
            recv_sem=line_recv.at[part, by],
            device_id=there,
            device_id_type=MESH,
        )

    def own_line(part):
        return pltpu.make_async_copy(
            grad_ref.at[:, pl.ds(STARTS[part], WIDTHS[part])],
            lines[part].at[pl.ds(pl.multiple_of(here[part] * 128, 128), 128)],
            local_sem.at[part],
        )

    def table_copy(part, by):
        target = moved(here, part, by)
        return pltpu.make_async_remote_copy(
            src_ref=tables.at[part, target[part]],
            dst_ref=got_tables.at[part, here[part]],
            send_sem=table_send.at[part, by],
            recv_sem=table_recv.at[part, by],
            device_id=place(target, core),
            device_id_type=MESH,
        )

    def own_table(part):
        return pltpu.make_async_copy(
            tables.at[part, here[part]], got_tables.at[part, here[part]], local_sem.at[3 + part]
        )

    for by in (1, 3, 2):
        for part in range(3):
            line_copy(part, by).start()
    for part in range(3):
        own_line(part).start()
    load_weight = pltpu.make_async_copy(weight_ref.at[0], weight, local_sem.at[6])
    load_weight.start()

    rollout = rollout_ref[...]
    token_weight = jnp.zeros((1, 128), jnp.float32)
    for i in range(4):
        hit = (rollout == i).astype(jnp.float32)
        count = jnp.sum(hit, axis=1, keepdims=True)
        token_weight = token_weight + hit * (adv_ref[:, i : i + 1] * 32.0 / count)
    scale = gate_ref[...] * token_weight
    route = route_ref[...]
    sooner = (
        lax.broadcasted_iota(jnp.int32, (128, 128), 0)
        < lax.broadcasted_iota(jnp.int32, (128, 128), 1)
    ).astype(jnp.bfloat16)
    for part in range(3):
        expert = expert_rows(part)
        named = jnp.zeros((128, 128), jnp.float32)
        held = jnp.zeros((128, 128), jnp.float32)
        for k in range(8):
            match = route[k : k + 1, :] == expert
            named = named + jnp.where(match, 1.0, 0.0)
            held = held + jnp.where(match, scale[k : k + 1, :], 0.0)
        rank = jnp.dot(named.astype(jnp.bfloat16), sooner, preferred_element_type=jnp.float32)
        rank = jnp.where(named > 0.5, rank, -1.0)
        for i in range(SIDE):
            tables[part, i, 0:32] = rank[32 * i : 32 * i + 32]
            tables[part, i, 32:64] = held[32 * i : 32 * i + 32]
    for by in (1, 3, 2):
        for part in range(3):
            table_copy(part, by).start()
    for part in range(3):
        own_table(part).start()

    def hidden_copy(index):
        group, owner = other(index)
        return pltpu.make_async_remote_copy(
            src_ref=answer.at[group * 32 + owner],
            dst_ref=got_hidden.at[me],
            send_sem=hidden_send.at[index],
            recv_sem=hidden_recv.at[index],
            device_id=(group, owner),
            device_id_type=MESH,
        )

    own_hidden = pltpu.make_async_copy(answer.at[me], got_hidden.at[me], local_sem.at[8])

    def gather(block, carry):
        wanted_spot = lax.broadcasted_iota(jnp.int32, (384, 1024), 0) + block * 384
        pick = jnp.where(wanted_spot == spot_ref[...], 1.0, 0.0).astype(jnp.bfloat16)
        found = jnp.dot(pick, hidden_ref[...], preferred_element_type=jnp.float32)
        for i in range(32):
            rows = found[i * CAP : i * CAP + CAP]
            rows = jnp.concatenate([rows[:, :384], rows[:, 384:]], axis=0)
            answer[block * 32 + i] = rows.astype(jnp.bfloat16)
        return carry

    lax.fori_loop(0, 4, gather, 0)
    own_hidden.start()

    def mid_copy(part, by):
        return pltpu.make_async_remote_copy(
            src_ref=sends[part].at[by],
            dst_ref=mids[part].at[by - 1],
            send_sem=mid_send.at[part, by],
            recv_sem=mid_recv.at[part, by],
            device_id=place(moved(here, (part + 1) % 3, by), core),
            device_id_type=MESH,
        )

    def last_copy(part, by, step, flip, source):
        second, third = (part + 1) % 3, (part + 2) % 3
        target = moved(here, third, step)
        there_core = (core + flip) % 2
        rows = pl.ds(pl.multiple_of((target[third] * 2 + there_core) * PICK, PICK), PICK)
        origin = (here[second] + SIDE - by) % SIDE
        block = here[third] * 2 + core
        return source.at[rows], outs[part].at[block, origin], target, there_core

    def last_remote(part, by, index, source):
        step, flip = index // 2, index % 2
        src, dst, target, there_core = last_copy(part, by, step, flip, source)
        return pltpu.make_async_remote_copy(
            src_ref=src,
            dst_ref=dst,
            send_sem=last_send.at[part, by, index],
            recv_sem=last_recv.at[part, by, index],
            device_id=place(target, there_core),
            device_id_type=MESH,
        )

    def last_local(part, by, source):
        src, dst, _, _ = last_copy(part, by, 0, 0, source)
        return pltpu.make_async_copy(src, dst, last_recv.at[part, by, 0])

    def forward(part, by, source):
        last_local(part, by, source).start()

        def body(index, carry):
            last_remote(part, by, index, source).start()
            return carry

        lax.fori_loop(1, 8, body, 0)

    row = lax.broadcasted_iota(jnp.int32, (PICK, 512), 0)
    lane = lax.broadcasted_iota(jnp.int32, (PICK, 512), 1)
    wanted = jnp.where(lane // 128 == row // CAP, row % CAP, -7).astype(jnp.float32)

    for part in range(3):
        own_line(part).wait()
        own_table(part).wait()
        for by in (1, 3, 2):
            line_copy(part, by).wait()
            table_copy(part, by).wait()

    for part in range(3):

        def select(i, carry, part=part):
            by = (i + 1) % SIDE
            target = (here[(part + 1) % 3] + by) % SIDE
            first = pl.multiple_of(target * 8, 8)
            ranks = jnp.concatenate(
                [got_tables[part, s, pl.ds(first, 8), :] for s in range(SIDE)], axis=1
            )
            helds = jnp.concatenate(
                [got_tables[part, s, pl.ds(first + 32, 8), :] for s in range(SIDE)], axis=1
            )
            scales = []
            for j in range(8):
                hit = ranks[j : j + 1, :] == wanted
                picks[pl.ds(j * PICK, PICK), :] = jnp.where(hit, 1.0, 0.0).astype(jnp.bfloat16)
                scales.append(
                    jnp.sum(jnp.where(hit, helds[j : j + 1, :], 0.0), axis=1, keepdims=True)
                )
            factor = jnp.concatenate(scales, axis=0)
            for start in range(0, WIDTHS[part], 256):
                width = min(256, WIDTHS[part] - start)
                found = jnp.dot(
                    picks[...],
                    lines[part][:, start : start + width],
                    preferred_element_type=jnp.float32,
                )
                sends[part][by, :, start : start + width] = (found * factor).astype(jnp.bfloat16)

            @pl.when(by > 0)
            def _():
                mid_copy(part, by).start()

            return carry

        lax.fori_loop(0, SIDE, select, 0)
        forward(part, 0, sends[part].at[0])

    def keep(part, by):
        origin = (here[(part + 1) % 3] + SIDE - by) % SIDE
        return pltpu.make_async_copy(
            outs[part].at[:, origin], kept[part].at[:, origin], keep_sem.at[part, by]
        )

    def absorb(part, by):
        last_local(part, by, mids[part].at[0]).wait()

        def arrive(index, carry):
            last_remote(part, by, index, mids[part].at[0]).wait_recv()
            return carry

        lax.fori_loop(1, 8, arrive, 0)
        keep(part, by).start()
        origin = (here[(part + 1) % 3] + SIDE - by) % SIDE
        rows = outs[part][:, origin].reshape(8 * PICK, WIDTHS[part])
        product = lax.dot_general(
            rows,
            weight[:, STARTS[part] : STARTS[part] + WIDTHS[part]],
            (((1,), (1,)), ((), ())),
            preferred_element_type=jnp.float32,
        )
        for block in range(8):
            for j in range(SIDE):
                coords = [None] * 3
                coords[part] = j
                coords[(part + 1) % 3] = origin
                coords[(part + 2) % 3] = block // 2
                group, owner = place(coords, block % 2)
                first = block * PICK + j * CAP
                device = group * 32 + owner
                total[device] = total[device] + product[first : first + CAP]

    total[...] = jnp.zeros_like(total)
    load_weight.wait()

    def push(index, carry):
        hidden_copy(index).start()
        return carry

    def onward(step, carry):
        @pl.when(step < SIDE)
        def _():
            for part in range(3):
                mid_copy(part, step).wait()
                forward(part, step, mids[part].at[step - 1])

        @pl.when(step < SIDE - 1)
        def _():
            lax.fori_loop(64 * step - 63, jnp.minimum(64 * step + 1, 128), push, 0)

        for part in range(3):
            absorb(part, step - 1)
        return carry

    lax.fori_loop(1, SIDE + 1, onward, 0)

    def settle(index, carry):
        hidden_copy(index).wait_send()
        return carry

    def collect(index, carry):
        hidden_copy(index).wait_recv()
        return carry

    own_hidden.wait()
    lax.fori_loop(1, 128, settle, 0)

    def pack(device, carry):
        rows = total[device]
        rows = jnp.concatenate([rows[:, :384], rows[:, 384:]], axis=0)
        answer[device] = rows.astype(jnp.bfloat16)
        return carry

    lax.fori_loop(0, 128, pack, 0)
    give = pltpu.make_async_copy(answer, answer_ref, local_sem.at[7])
    give.start()

    for part in range(3):

        def finish(i, carry, part=part):
            keep(part, i).wait()

            def body(index, inner):
                last_remote(part, i, index, mids[part].at[0]).wait_send()
                return inner

            return lax.fori_loop(1, 8, body, carry)

        lax.fori_loop(0, SIDE, finish, 0)
    lax.fori_loop(1, 128, collect, 0)
    give.wait()


def dispatch(*operands):
    vmem = pl.BlockSpec(memory_space=pltpu.VMEM)
    hbm = pl.BlockSpec(memory_space=pl.ANY)
    scratch = [
        pltpu.VMEM((768, 4096), jnp.bfloat16),
        pltpu.VMEM((128, CAP, 768), jnp.float32),
        pltpu.VMEM((128, 2 * CAP, 384), jnp.bfloat16),
    ]
    scratch += [pltpu.VMEM((8, SIDE, PICK, w), jnp.bfloat16) for w in WIDTHS]
    scratch += [pltpu.VMEM((512, w), jnp.bfloat16) for w in WIDTHS]
    scratch += [
        pltpu.VMEM((3, SIDE, 64, 128), jnp.float32),
        pltpu.VMEM((3, SIDE, 64, 128), jnp.float32),
        pltpu.VMEM((8 * PICK, 512), jnp.bfloat16),
    ]
    scratch += [pltpu.VMEM((SIDE, 8 * PICK, w), jnp.bfloat16) for w in WIDTHS]
    scratch += [pltpu.VMEM((SIDE - 1, 8 * PICK, w), jnp.bfloat16) for w in WIDTHS]
    scratch += [pltpu.SemaphoreType.DMA((9,))]
    scratch += [pltpu.SemaphoreType.DMA((3, SIDE)) for _ in range(7)]
    scratch += [pltpu.SemaphoreType.DMA((3, SIDE, 8)) for _ in range(2)]
    scratch += [pltpu.SemaphoreType.DMA((128,)) for _ in range(2)]
    shapes = [jax.ShapeDtypeStruct((8, SIDE, PICK, w), jnp.bfloat16) for w in WIDTHS]
    shapes += [jax.ShapeDtypeStruct((128, 2 * CAP, 384), jnp.bfloat16)] * 2
    return pl.pallas_call(
        dispatch_kernel,
        out_shape=shapes,
        in_specs=[vmem] * 7 + [hbm],
        out_specs=[hbm] * 5,
        scratch_shapes=scratch,
        compiler_params=pltpu.CompilerParams(
            collective_id=0, has_side_effects=True, vmem_limit_bytes=62 << 20
        ),
    )(*operands)


def arrange_kernel(got_ref, *out_refs):
    for part in range(3):

        def block_of(block, carry, part=part):
            pieces = []
            for j in range(SIDE):
                coords = [None] * 3
                coords[part] = j
                coords[(part + 1) % 3] = block % SIDE
                coords[(part + 2) % 3] = block // 8
                group, owner = place(coords, (block // SIDE) % 2)
                rows = got_ref[group * 32 + owner].astype(jnp.float32)
                pieces.append(jnp.concatenate([rows[:CAP], rows[CAP:]], axis=1))
            first = pl.multiple_of(block * PICK, PICK)
            out_refs[part][pl.ds(first, PICK)] = jnp.concatenate(pieces, axis=0).astype(
                jnp.bfloat16
            )
            return carry

        lax.fori_loop(0, 32, block_of, 0)


def arrange(got):
    vmem = pl.BlockSpec(memory_space=pltpu.VMEM)
    return pl.pallas_call(
        arrange_kernel,
        out_shape=[jax.ShapeDtypeStruct((1536, 768), jnp.bfloat16)] * 3,
        in_specs=[vmem],
        out_specs=[vmem] * 3,
        compiler_params=pltpu.CompilerParams(vmem_limit_bytes=24 << 20),
        cost_estimate=pl.CostEstimate(flops=0, bytes_accessed=10 << 20, transcendentals=0),
    )(got)


def shards(hidden, out_grad, route_ids, gate_vals, rollout_ids, advantages, down_weight):
    slots = 1024
    named = jnp.sum(
        (route_ids[:, :, None] == jnp.arange(128, dtype=jnp.int32)).astype(jnp.bfloat16), axis=1
    )
    t = jnp.arange(128, dtype=jnp.int32)
    earlier = (t[:, None] > t[None, :]).astype(jnp.bfloat16)
    before = jnp.dot(earlier, named, preferred_element_type=jnp.float32)
    rank = jnp.sum(
        jnp.where(
            route_ids[:, :, None] == jnp.arange(128, dtype=jnp.int32), before[:, None, :], 0.0
        ),
        axis=2,
    ).astype(jnp.int32)
    spot = (route_ids * CAP + rank).reshape(slots)
    one_hot = (jnp.arange(1536, dtype=jnp.int32)[:, None] == spot[None, :]).astype(jnp.bfloat16)

    parts = dispatch(
        route_ids.T,
        gate_vals.T,
        rollout_ids,
        advantages,
        out_grad,
        spot[None, :],
        hidden.reshape(slots, 768),
        down_weight,
    )

    def exchange(rows):
        return lax.all_to_all(rows, ("grp", "ep"), split_axis=0, concat_axis=0, tiled=True)

    got_hidden = parts[4]
    returned = exchange(parts[3])
    grads = [
        lax.dot_general(
            rows,
            part.reshape(1536, width),
            (((0,), (0,)), ((), ())),
            preferred_element_type=jnp.float32,
        ).astype(jnp.bfloat16)
        for rows, part, width in zip(arrange(got_hidden), parts[:3], WIDTHS)
    ]
    weight_grad = jnp.concatenate(grads, axis=1)
    returned = returned.reshape(128, 2, CAP, 384).transpose(0, 2, 1, 3).reshape(1536, 768)
    hidden_grad = lax.dot_general(
        one_hot, returned, (((0,), (0,)), ((), ())), preferred_element_type=jnp.float32
    ).astype(jnp.bfloat16)
    return hidden_grad.reshape(128, 8, 768), weight_grad[None]


def solution(mesh):
    wide = P(("grp", "ep"), None, None)
    flat = P(("grp", "ep"), None)
    return jax.shard_map(
        shards,
        mesh=mesh,
        in_specs=(wide, flat, flat, flat, flat, flat, wide),
        out_specs=(wide, wide),
        check_vma=False,
    )
```

```python
import jax
import jax.numpy as jnp
from jax import lax
from jax.experimental import pallas as pl
from jax.experimental.pallas import tpu as pltpu
from jax.sharding import PartitionSpec as P

MESH = pl.DeviceIdType.MESH
SIDE = 4
CAP = 12
STRIDE = 77
PICK = SIDE * CAP
WIDTHS = (1280, 1280, 1536)
STARTS = (0, 1280, 2560)


def position():
    group, owner = lax.axis_index("grp"), lax.axis_index("ep")
    core = group % 2
    z = (group // 2) * 2 + owner % 2
    x = (owner // 2) % 4
    y = owner // 8
    return (x, y, z), core


def place(coords, core):
    x, y, z = coords
    return ((z // 2) * 2 + core, y * 8 + x * 2 + z % 2)


def moved(coords, axis, by):
    new = list(coords)
    new[axis] = (coords[axis] + by) % SIDE
    return tuple(new)


def expert_rows(part):
    row = lax.broadcasted_iota(jnp.int32, (128, 128), 0)
    coords = [None] * 3
    coords[part % 3] = row // 32
    coords[(part + 1) % 3] = (row // 8) % 4
    coords[(part + 2) % 3] = (row // 2) % 4
    x, y, z = coords
    return ((z // 2) * 2 + row % 2) * 32 + y * 8 + x * 2 + z % 2


def dispatch_kernel(
    route_ref,
    gate_ref,
    rollout_ref,
    adv_ref,
    grad_ref,
    spot_ref,
    hidden_ref,
    weight_ref,
    kept0,
    kept1,
    kept2,
    answer_ref,
    got_hidden,
    weight,
    total,
    answer,
    out0,
    out1,
    out2,
    lines0,
    lines1,
    lines2,
    tables,
    got_tables,
    picks,
    send0,
    send1,
    send2,
    mid0,
    mid1,
    mid2,
    local_sem,
    keep_sem,
    line_send,
    line_recv,
    table_send,
    table_recv,
    mid_send,
    mid_recv,
    last_send,
    last_recv,
    hidden_send,
    hidden_recv,
):
    outs, lines = (out0, out1, out2), (lines0, lines1, lines2)
    kept = (kept0, kept1, kept2)
    sends, mids = (send0, send1, send2), (mid0, mid1, mid2)
    here, core = position()

    barrier = pltpu.get_barrier_semaphore()
    me = lax.axis_index("grp") * 32 + lax.axis_index("ep")

    def other(index):
        shift = (index * STRIDE) & 127
        x, y, z = here
        x, y, z = (x + (shift >> 1)) & 3, (y + (shift >> 3)) & 3, (z + (shift >> 5)) & 3
        return ((z & 2) + ((core + shift) & 1), y * 8 + x * 2 + (z & 1))

    def greet(index, carry):
        pl.semaphore_signal(barrier, inc=1, device_id=other(index), device_id_type=MESH)
        return carry

    lax.fori_loop(1, 128, greet, 0)
    pl.semaphore_wait(barrier, 127)

    def line_copy(part, by):
        there = place(moved(here, part, by), core)
        return pltpu.make_async_remote_copy(
            src_ref=grad_ref.at[:, pl.ds(STARTS[part], WIDTHS[part])],
            dst_ref=lines[part].at[pl.ds(pl.multiple_of(here[part] * 128, 128), 128)],
            send_sem=line_send.at[part, by],
            recv_sem=line_recv.at[part, by],
            device_id=there,
            device_id_type=MESH,
        )

    def own_line(part):
        return pltpu.make_async_copy(
            grad_ref.at[:, pl.ds(STARTS[part], WIDTHS[part])],
            lines[part].at[pl.ds(pl.multiple_of(here[part] * 128, 128), 128)],
            local_sem.at[part],
        )

    def table_copy(part, by):
        target = moved(here, part, by)
        return pltpu.make_async_remote_copy(
            src_ref=tables.at[part, target[part]],
            dst_ref=got_tables.at[part, here[part]],
            send_sem=table_send.at[part, by],
            recv_sem=table_recv.at[part, by],
            device_id=place(target, core),
            device_id_type=MESH,
        )

    def own_table(part):
        return pltpu.make_async_copy(
            tables.at[part, here[part]], got_tables.at[part, here[part]], local_sem.at[3 + part]
        )

    for by in (1, 3, 2):
        for part in range(3):
            line_copy(part, by).start()
    for part in range(3):
        own_line(part).start()
    load_weight = pltpu.make_async_copy(weight_ref.at[0], weight, local_sem.at[6])
    load_weight.start()

    rollout = rollout_ref[...]
    token_weight = jnp.zeros((1, 128), jnp.float32)
    for i in range(4):
        hit = (rollout == i).astype(jnp.float32)
        count = jnp.sum(hit, axis=1, keepdims=True)
        token_weight = token_weight + hit * (adv_ref[:, i : i + 1] * 32.0 / count)
    scale = gate_ref[...] * token_weight
    route = route_ref[...]
    sooner = (
        lax.broadcasted_iota(jnp.int32, (128, 128), 0)
        < lax.broadcasted_iota(jnp.int32, (128, 128), 1)
    ).astype(jnp.bfloat16)
    for part in range(3):
        expert = expert_rows(part)
        named = jnp.zeros((128, 128), jnp.float32)
        held = jnp.zeros((128, 128), jnp.float32)
        for k in range(8):
            match = route[k : k + 1, :] == expert
            named = named + jnp.where(match, 1.0, 0.0)
            held = held + jnp.where(match, scale[k : k + 1, :], 0.0)
        rank = jnp.dot(named.astype(jnp.bfloat16), sooner, preferred_element_type=jnp.float32)
        rank = jnp.where(named > 0.5, rank, -1.0)
        for i in range(SIDE):
            tables[part, i, 0:32] = rank[32 * i : 32 * i + 32]
            tables[part, i, 32:64] = held[32 * i : 32 * i + 32]
    for by in (1, 3, 2):
        for part in range(3):
            table_copy(part, by).start()
    for part in range(3):
        own_table(part).start()

    def hidden_copy(index):
        group, owner = other(index)
        return pltpu.make_async_remote_copy(
            src_ref=answer.at[group * 32 + owner],
            dst_ref=got_hidden.at[me],
            send_sem=hidden_send.at[index],
            recv_sem=hidden_recv.at[index],
            device_id=(group, owner),
            device_id_type=MESH,
        )

    own_hidden = pltpu.make_async_copy(answer.at[me], got_hidden.at[me], local_sem.at[8])

    def gather(block, carry):
        wanted_spot = lax.broadcasted_iota(jnp.int32, (384, 1024), 0) + block * 384
        pick = jnp.where(wanted_spot == spot_ref[...], 1.0, 0.0).astype(jnp.bfloat16)
        found = jnp.dot(pick, hidden_ref[...], preferred_element_type=jnp.float32)
        for i in range(32):
            rows = found[i * CAP : i * CAP + CAP]
            rows = jnp.concatenate([rows[:, :384], rows[:, 384:]], axis=0)
            answer[block * 32 + i] = rows.astype(jnp.bfloat16)
        return carry

    lax.fori_loop(0, 4, gather, 0)
    own_hidden.start()

    def mid_copy(part, by):
        return pltpu.make_async_remote_copy(
            src_ref=sends[part].at[by],
            dst_ref=mids[part].at[by - 1],
            send_sem=mid_send.at[part, by],
            recv_sem=mid_recv.at[part, by],
            device_id=place(moved(here, (part + 1) % 3, by), core),
            device_id_type=MESH,
        )

    def last_copy(part, by, step, flip, source):
        second, third = (part + 1) % 3, (part + 2) % 3
        target = moved(here, third, step)
        there_core = (core + flip) % 2
        rows = pl.ds(pl.multiple_of((target[third] * 2 + there_core) * PICK, PICK), PICK)
        origin = (here[second] + SIDE - by) % SIDE
        block = here[third] * 2 + core
        return source.at[rows], outs[part].at[block, origin], target, there_core

    def last_remote(part, by, index, source):
        step, flip = index // 2, index % 2
        src, dst, target, there_core = last_copy(part, by, step, flip, source)
        return pltpu.make_async_remote_copy(
            src_ref=src,
            dst_ref=dst,
            send_sem=last_send.at[part, by, index],
            recv_sem=last_recv.at[part, by, index],
            device_id=place(target, there_core),
            device_id_type=MESH,
        )

    def last_local(part, by, source):
        src, dst, _, _ = last_copy(part, by, 0, 0, source)
        return pltpu.make_async_copy(src, dst, last_recv.at[part, by, 0])

    def forward(part, by, source):
        last_local(part, by, source).start()

        def body(index, carry):
            last_remote(part, by, index, source).start()
            return carry

        lax.fori_loop(1, 8, body, 0)

    row = lax.broadcasted_iota(jnp.int32, (PICK, 512), 0)
    lane = lax.broadcasted_iota(jnp.int32, (PICK, 512), 1)
    wanted = jnp.where(lane // 128 == row // CAP, row % CAP, -7).astype(jnp.float32)

    for part in range(3):
        own_line(part).wait()
        own_table(part).wait()
        for by in (1, 3, 2):
            line_copy(part, by).wait()
            table_copy(part, by).wait()

    for part in range(3):

        def select(i, carry, part=part):
            by = (i + 1) % SIDE
            target = (here[(part + 1) % 3] + by) % SIDE
            first = pl.multiple_of(target * 8, 8)
            ranks = jnp.concatenate(
                [got_tables[part, s, pl.ds(first, 8), :] for s in range(SIDE)], axis=1
            )
            helds = jnp.concatenate(
                [got_tables[part, s, pl.ds(first + 32, 8), :] for s in range(SIDE)], axis=1
            )
            scales = []
            for j in range(8):
                hit = ranks[j : j + 1, :] == wanted
                picks[pl.ds(j * PICK, PICK), :] = jnp.where(hit, 1.0, 0.0).astype(jnp.bfloat16)
                scales.append(
                    jnp.sum(jnp.where(hit, helds[j : j + 1, :], 0.0), axis=1, keepdims=True)
                )
            factor = jnp.concatenate(scales, axis=0)
            for start in range(0, WIDTHS[part], 256):
                width = min(256, WIDTHS[part] - start)
                found = jnp.dot(
                    picks[...],
                    lines[part][:, start : start + width],
                    preferred_element_type=jnp.float32,
                )
                sends[part][by, :, start : start + width] = (found * factor).astype(jnp.bfloat16)

            @pl.when(by > 0)
            def _():
                mid_copy(part, by).start()

            return carry

        lax.fori_loop(0, SIDE, select, 0)
        forward(part, 0, sends[part].at[0])

    def keep(part, by):
        origin = (here[(part + 1) % 3] + SIDE - by) % SIDE
        return pltpu.make_async_copy(
            outs[part].at[:, origin], kept[part].at[:, origin], keep_sem.at[part, by]
        )

    def absorb(part, by):
        last_local(part, by, mids[part].at[0]).wait()

        def arrive(index, carry):
            last_remote(part, by, index, mids[part].at[0]).wait_recv()
            return carry

        lax.fori_loop(1, 8, arrive, 0)
        keep(part, by).start()
        origin = (here[(part + 1) % 3] + SIDE - by) % SIDE
        rows = outs[part][:, origin].reshape(8 * PICK, WIDTHS[part])
        product = lax.dot_general(
            rows,
            weight[:, STARTS[part] : STARTS[part] + WIDTHS[part]],
            (((1,), (1,)), ((), ())),
            preferred_element_type=jnp.float32,
        )
        for block in range(8):
            for j in range(SIDE):
                coords = [None] * 3
                coords[part] = j
                coords[(part + 1) % 3] = origin
                coords[(part + 2) % 3] = block // 2
                group, owner = place(coords, block % 2)
                first = block * PICK + j * CAP
                device = group * 32 + owner
                total[device] = total[device] + product[first : first + CAP]

    total[...] = jnp.zeros_like(total)
    load_weight.wait()

    def push(index, carry):
        hidden_copy(index).start()
        return carry

    def onward(step, carry):
        @pl.when(step < SIDE)
        def _():
            for part in range(3):
                mid_copy(part, step).wait()
                forward(part, step, mids[part].at[step - 1])

        @pl.when(step < SIDE - 1)
        def _():
            lax.fori_loop(64 * step - 63, jnp.minimum(64 * step + 1, 128), push, 0)

        for part in range(3):
            absorb(part, step - 1)
        return carry

    lax.fori_loop(1, SIDE + 1, onward, 0)

    def settle(index, carry):
        hidden_copy(index).wait_send()
        return carry

    def collect(index, carry):
        hidden_copy(index).wait_recv()
        return carry

    own_hidden.wait()
    lax.fori_loop(1, 128, settle, 0)

    def pack(device, carry):
        rows = total[device]
        rows = jnp.concatenate([rows[:, :384], rows[:, 384:]], axis=0)
        answer[device] = rows.astype(jnp.bfloat16)
        return carry

    lax.fori_loop(0, 128, pack, 0)
    give = pltpu.make_async_copy(answer, answer_ref, local_sem.at[7])
    give.start()

    for part in range(3):

        def finish(i, carry, part=part):
            keep(part, i).wait()

            def body(index, inner):
                last_remote(part, i, index, mids[part].at[0]).wait_send()
                return inner

            return lax.fori_loop(1, 8, body, carry)

        lax.fori_loop(0, SIDE, finish, 0)
    lax.fori_loop(1, 128, collect, 0)
    give.wait()


def dispatch(*operands):
    vmem = pl.BlockSpec(memory_space=pltpu.VMEM)
    hbm = pl.BlockSpec(memory_space=pl.ANY)
    scratch = [
        pltpu.VMEM((768, 4096), jnp.bfloat16),
        pltpu.VMEM((128, CAP, 768), jnp.float32),
        pltpu.VMEM((128, 2 * CAP, 384), jnp.bfloat16),
    ]
    scratch += [pltpu.VMEM((8, SIDE, PICK, w), jnp.bfloat16) for w in WIDTHS]
    scratch += [pltpu.VMEM((512, w), jnp.bfloat16) for w in WIDTHS]
    scratch += [
        pltpu.VMEM((3, SIDE, 64, 128), jnp.float32),
        pltpu.VMEM((3, SIDE, 64, 128), jnp.float32),
        pltpu.VMEM((8 * PICK, 512), jnp.bfloat16),
    ]
    scratch += [pltpu.VMEM((SIDE, 8 * PICK, w), jnp.bfloat16) for w in WIDTHS]
    scratch += [pltpu.VMEM((SIDE - 1, 8 * PICK, w), jnp.bfloat16) for w in WIDTHS]
    scratch += [pltpu.SemaphoreType.DMA((9,))]
    scratch += [pltpu.SemaphoreType.DMA((3, SIDE)) for _ in range(7)]
    scratch += [pltpu.SemaphoreType.DMA((3, SIDE, 8)) for _ in range(2)]
    scratch += [pltpu.SemaphoreType.DMA((128,)) for _ in range(2)]
    shapes = [jax.ShapeDtypeStruct((8, SIDE, PICK, w), jnp.bfloat16) for w in WIDTHS]
    shapes += [jax.ShapeDtypeStruct((128, 2 * CAP, 384), jnp.bfloat16)] * 2
    return pl.pallas_call(
        dispatch_kernel,
        out_shape=shapes,
        in_specs=[vmem] * 7 + [hbm],
        out_specs=[hbm] * 5,
        scratch_shapes=scratch,
        compiler_params=pltpu.CompilerParams(
            collective_id=0, has_side_effects=True, vmem_limit_bytes=62 << 20
        ),
    )(*operands)


def arrange_kernel(got_ref, *out_refs):
    for part in range(3):

        def block_of(block, carry, part=part):
            pieces = []
            for j in range(SIDE):
                coords = [None] * 3
                coords[part] = j
                coords[(part + 1) % 3] = block % SIDE
                coords[(part + 2) % 3] = block // 8
                group, owner = place(coords, (block // SIDE) % 2)
                rows = got_ref[group * 32 + owner].astype(jnp.float32)
                pieces.append(jnp.concatenate([rows[:CAP], rows[CAP:]], axis=1))
            first = pl.multiple_of(block * PICK, PICK)
            out_refs[part][pl.ds(first, PICK)] = jnp.concatenate(pieces, axis=0).astype(
                jnp.bfloat16
            )
            return carry

        lax.fori_loop(0, 32, block_of, 0)


def arrange(got):
    vmem = pl.BlockSpec(memory_space=pltpu.VMEM)
    return pl.pallas_call(
        arrange_kernel,
        out_shape=[jax.ShapeDtypeStruct((1536, 768), jnp.bfloat16)] * 3,
        in_specs=[vmem],
        out_specs=[vmem] * 3,
        compiler_params=pltpu.CompilerParams(vmem_limit_bytes=24 << 20),
        cost_estimate=pl.CostEstimate(flops=0, bytes_accessed=10 << 20, transcendentals=0),
    )(got)


def restore_kernel(spot_ref, got_ref, out_ref, rows):
    def stage(block, carry):
        pieces = []
        for j in range(SIDE):
            piece = got_ref[block * SIDE + j].astype(jnp.float32)
            pieces.append(jnp.concatenate([piece[:CAP], piece[CAP:]], axis=1))
        first = pl.multiple_of(block * PICK, PICK)
        rows[pl.ds(first, PICK)] = jnp.concatenate(pieces, axis=0).astype(jnp.bfloat16)
        return carry

    lax.fori_loop(0, 32, stage, 0)
    for first in range(0, 1024, 256):
        place_of = lax.broadcasted_iota(jnp.int32, (256, 1536), 1)
        pick = jnp.where(spot_ref[first : first + 256] == place_of, 1.0, 0.0)
        out_ref[first : first + 256] = jnp.dot(
            pick.astype(jnp.bfloat16), rows[...], preferred_element_type=jnp.float32
        ).astype(jnp.bfloat16)


def restore(spot, got):
    vmem = pl.BlockSpec(memory_space=pltpu.VMEM)
    return pl.pallas_call(
        restore_kernel,
        out_shape=jax.ShapeDtypeStruct((1024, 768), jnp.bfloat16),
        in_specs=[vmem] * 2,
        out_specs=vmem,
        scratch_shapes=[pltpu.VMEM((1536, 768), jnp.bfloat16)],
        compiler_params=pltpu.CompilerParams(vmem_limit_bytes=24 << 20),
    )(spot, got)


def shards(hidden, out_grad, route_ids, gate_vals, rollout_ids, advantages, down_weight):
    slots = 1024
    named = jnp.sum(
        (route_ids[:, :, None] == jnp.arange(128, dtype=jnp.int32)).astype(jnp.bfloat16), axis=1
    )
    t = jnp.arange(128, dtype=jnp.int32)
    earlier = (t[:, None] > t[None, :]).astype(jnp.bfloat16)
    before = jnp.dot(earlier, named, preferred_element_type=jnp.float32)
    rank = jnp.sum(
        jnp.where(
            route_ids[:, :, None] == jnp.arange(128, dtype=jnp.int32), before[:, None, :], 0.0
        ),
        axis=2,
    ).astype(jnp.int32)
    spot = (route_ids * CAP + rank).reshape(slots)

    parts = dispatch(
        route_ids.T,
        gate_vals.T,
        rollout_ids,
        advantages,
        out_grad,
        spot[None, :],
        hidden.reshape(slots, 768),
        down_weight,
    )

    def exchange(rows):
        return lax.all_to_all(rows, ("grp", "ep"), split_axis=0, concat_axis=0, tiled=True)

    got_hidden = parts[4]
    returned = exchange(parts[3])
    grads = [
        lax.dot_general(
            rows,
            part.reshape(1536, width),
            (((0,), (0,)), ((), ())),
            preferred_element_type=jnp.float32,
        ).astype(jnp.bfloat16)
        for rows, part, width in zip(arrange(got_hidden), parts[:3], WIDTHS)
    ]
    weight_grad = jnp.concatenate(grads, axis=1)
    hidden_grad = restore(spot[:, None], returned)
    return hidden_grad.reshape(128, 8, 768), weight_grad[None]


def solution(mesh):
    wide = P(("grp", "ep"), None, None)
    flat = P(("grp", "ep"), None)
    return jax.shard_map(
        shards,
        mesh=mesh,
        in_specs=(wide, flat, flat, flat, flat, flat, wide),
        out_specs=(wide, wide),
        check_vma=False,
    )
```

```python
import jax
import jax.numpy as jnp
from jax import lax
from jax.experimental import pallas as pl
from jax.experimental.pallas import tpu as pltpu
from jax.sharding import PartitionSpec as P

MESH = pl.DeviceIdType.MESH
SIDE = 4
CAP = 12
STRIDE = 77
PICK = SIDE * CAP
WIDTHS = (1280, 1280, 1536)
STARTS = (0, 1280, 2560)


def position():
    group, owner = lax.axis_index("grp"), lax.axis_index("ep")
    core = group % 2
    z = (group // 2) * 2 + owner % 2
    x = (owner // 2) % 4
    y = owner // 8
    return (x, y, z), core


def place(coords, core):
    x, y, z = coords
    return ((z // 2) * 2 + core, y * 8 + x * 2 + z % 2)


def moved(coords, axis, by):
    new = list(coords)
    new[axis] = (coords[axis] + by) % SIDE
    return tuple(new)


def expert_rows(part):
    row = lax.broadcasted_iota(jnp.int32, (128, 128), 0)
    coords = [None] * 3
    coords[part % 3] = row // 32
    coords[(part + 1) % 3] = (row // 8) % 4
    coords[(part + 2) % 3] = (row // 2) % 4
    x, y, z = coords
    return ((z // 2) * 2 + row % 2) * 32 + y * 8 + x * 2 + z % 2


def dispatch_kernel(
    route_ref,
    gate_ref,
    rollout_ref,
    adv_ref,
    grad_ref,
    spot_ref,
    hidden_ref,
    weight_ref,
    kept0,
    kept1,
    kept2,
    answer_ref,
    got_hidden,
    weight,
    total,
    answer,
    out0,
    out1,
    out2,
    lines0,
    lines1,
    lines2,
    tables,
    got_tables,
    picks,
    send0,
    send1,
    send2,
    mid0,
    mid1,
    mid2,
    local_sem,
    keep_sem,
    line_send,
    line_recv,
    table_send,
    table_recv,
    mid_send,
    mid_recv,
    last_send,
    last_recv,
    hidden_send,
    hidden_recv,
):
    outs, lines = (out0, out1, out2), (lines0, lines1, lines2)
    kept = (kept0, kept1, kept2)
    sends, mids = (send0, send1, send2), (mid0, mid1, mid2)
    here, core = position()

    barrier = pltpu.get_barrier_semaphore()
    me = lax.axis_index("grp") * 32 + lax.axis_index("ep")

    def other(index):
        shift = (index * STRIDE) & 127
        x, y, z = here
        x, y, z = (x + (shift >> 1)) & 3, (y + (shift >> 3)) & 3, (z + (shift >> 5)) & 3
        return ((z & 2) + ((core + shift) & 1), y * 8 + x * 2 + (z & 1))

    def greet(index, carry):
        pl.semaphore_signal(barrier, inc=1, device_id=other(index), device_id_type=MESH)
        return carry

    lax.fori_loop(1, 128, greet, 0)
    pl.semaphore_wait(barrier, 127)

    def line_copy(part, by):
        there = place(moved(here, part, by), core)
        return pltpu.make_async_remote_copy(
            src_ref=grad_ref.at[:, pl.ds(STARTS[part], WIDTHS[part])],
            dst_ref=lines[part].at[pl.ds(pl.multiple_of(here[part] * 128, 128), 128)],
            send_sem=line_send.at[part, by],
            recv_sem=line_recv.at[part, by],
            device_id=there,
            device_id_type=MESH,
        )

    def own_line(part):
        return pltpu.make_async_copy(
            grad_ref.at[:, pl.ds(STARTS[part], WIDTHS[part])],
            lines[part].at[pl.ds(pl.multiple_of(here[part] * 128, 128), 128)],
            local_sem.at[part],
        )

    def table_copy(part, by):
        target = moved(here, part, by)
        return pltpu.make_async_remote_copy(
            src_ref=tables.at[part, target[part]],
            dst_ref=got_tables.at[part, here[part]],
            send_sem=table_send.at[part, by],
            recv_sem=table_recv.at[part, by],
            device_id=place(target, core),
            device_id_type=MESH,
        )

    def own_table(part):
        return pltpu.make_async_copy(
            tables.at[part, here[part]], got_tables.at[part, here[part]], local_sem.at[3 + part]
        )

    for by in (1, 3, 2):
        for part in range(3):
            line_copy(part, by).start()
    for part in range(3):
        own_line(part).start()
    load_weight = pltpu.make_async_copy(weight_ref.at[0], weight, local_sem.at[6])
    load_weight.start()

    rollout = rollout_ref[...]
    token_weight = jnp.zeros((1, 128), jnp.float32)
    for i in range(4):
        hit = (rollout == i).astype(jnp.float32)
        count = jnp.sum(hit, axis=1, keepdims=True)
        token_weight = token_weight + hit * (adv_ref[:, i : i + 1] * 32.0 / count)
    scale = gate_ref[...] * token_weight
    route = route_ref[...]
    sooner = (
        lax.broadcasted_iota(jnp.int32, (128, 128), 0)
        < lax.broadcasted_iota(jnp.int32, (128, 128), 1)
    ).astype(jnp.bfloat16)
    for part in range(3):
        expert = expert_rows(part)
        named = jnp.zeros((128, 128), jnp.float32)
        held = jnp.zeros((128, 128), jnp.float32)
        for k in range(8):
            match = route[k : k + 1, :] == expert
            named = named + jnp.where(match, 1.0, 0.0)
            held = held + jnp.where(match, scale[k : k + 1, :], 0.0)
        rank = jnp.dot(named.astype(jnp.bfloat16), sooner, preferred_element_type=jnp.float32)
        rank = jnp.where(named > 0.5, rank, -1.0)
        for i in range(SIDE):
            tables[part, i, 0:32] = rank[32 * i : 32 * i + 32]
            tables[part, i, 32:64] = held[32 * i : 32 * i + 32]
    for by in (1, 3, 2):
        for part in range(3):
            table_copy(part, by).start()
    for part in range(3):
        own_table(part).start()

    def hidden_copy(index):
        group, owner = other(index)
        return pltpu.make_async_remote_copy(
            src_ref=answer.at[group * 32 + owner],
            dst_ref=got_hidden.at[me],
            send_sem=hidden_send.at[index],
            recv_sem=hidden_recv.at[index],
            device_id=(group, owner),
            device_id_type=MESH,
        )

    own_hidden = pltpu.make_async_copy(answer.at[me], got_hidden.at[me], local_sem.at[8])

    def gather(block, carry):
        wanted_spot = lax.broadcasted_iota(jnp.int32, (384, 1024), 0) + block * 384
        pick = jnp.where(wanted_spot == spot_ref[...], 1.0, 0.0).astype(jnp.bfloat16)
        found = jnp.dot(pick, hidden_ref[...], preferred_element_type=jnp.float32)
        for i in range(32):
            rows = found[i * CAP : i * CAP + CAP]
            rows = jnp.concatenate([rows[:, :384], rows[:, 384:]], axis=0)
            answer[block * 32 + i] = rows.astype(jnp.bfloat16)
        return carry

    lax.fori_loop(0, 4, gather, 0)
    own_hidden.start()

    def mid_copy(part, by):
        return pltpu.make_async_remote_copy(
            src_ref=sends[part].at[by],
            dst_ref=mids[part].at[by - 1],
            send_sem=mid_send.at[part, by],
            recv_sem=mid_recv.at[part, by],
            device_id=place(moved(here, (part + 1) % 3, by), core),
            device_id_type=MESH,
        )

    def last_copy(part, by, step, flip, source):
        second, third = (part + 1) % 3, (part + 2) % 3
        target = moved(here, third, step)
        there_core = (core + flip) % 2
        rows = pl.ds(pl.multiple_of((target[third] * 2 + there_core) * PICK, PICK), PICK)
        origin = (here[second] + SIDE - by) % SIDE
        block = here[third] * 2 + core
        return source.at[rows], outs[part].at[block, origin], target, there_core

    def last_remote(part, by, index, source):
        step, flip = index // 2, index % 2
        src, dst, target, there_core = last_copy(part, by, step, flip, source)
        return pltpu.make_async_remote_copy(
            src_ref=src,
            dst_ref=dst,
            send_sem=last_send.at[part, by, index],
            recv_sem=last_recv.at[part, by, index],
            device_id=place(target, there_core),
            device_id_type=MESH,
        )

    def last_local(part, by, source):
        src, dst, _, _ = last_copy(part, by, 0, 0, source)
        return pltpu.make_async_copy(src, dst, last_recv.at[part, by, 0])

    def forward(by, sources):
        for part in range(3):
            last_local(part, by, sources[part]).start()

        def body(index, carry):
            for part in range(3):
                last_remote(part, by, (3 * index) & 7, sources[part]).start()
            return carry

        lax.fori_loop(1, 8, body, 0)

    row = lax.broadcasted_iota(jnp.int32, (PICK, 512), 0)
    lane = lax.broadcasted_iota(jnp.int32, (PICK, 512), 1)
    wanted = jnp.where(lane // 128 == row // CAP, row % CAP, -7).astype(jnp.float32)

    for part in range(3):
        own_line(part).wait()
        own_table(part).wait()
        for by in (1, 3, 2):
            line_copy(part, by).wait()
            table_copy(part, by).wait()

    def select(i, carry):
        by = jnp.where(i < 2, 2 * i + 1, 6 - 2 * i)
        for part in range(3):
            target = (here[(part + 1) % 3] + by) % SIDE
            first = pl.multiple_of(target * 8, 8)
            ranks = jnp.concatenate(
                [got_tables[part, s, pl.ds(first, 8), :] for s in range(SIDE)], axis=1
            )
            helds = jnp.concatenate(
                [got_tables[part, s, pl.ds(first + 32, 8), :] for s in range(SIDE)], axis=1
            )
            scales = []
            for j in range(8):
                hit = ranks[j : j + 1, :] == wanted
                picks[pl.ds(j * PICK, PICK), :] = jnp.where(hit, 1.0, 0.0).astype(jnp.bfloat16)
                scales.append(
                    jnp.sum(jnp.where(hit, helds[j : j + 1, :], 0.0), axis=1, keepdims=True)
                )
            factor = jnp.concatenate(scales, axis=0)
            for start in range(0, WIDTHS[part], 256):
                found = jnp.dot(
                    picks[...],
                    lines[part][:, start : start + 256],
                    preferred_element_type=jnp.float32,
                )
                sends[part][by, :, start : start + 256] = (found * factor).astype(jnp.bfloat16)

            @pl.when(by > 0)
            def _():
                mid_copy(part, by).start()

        return carry

    lax.fori_loop(0, SIDE, select, 0)
    forward(0, [sends[part].at[0] for part in range(3)])

    def keep(part, by):
        origin = (here[(part + 1) % 3] + SIDE - by) % SIDE
        return pltpu.make_async_copy(
            outs[part].at[:, origin], kept[part].at[:, origin], keep_sem.at[part, by]
        )

    def absorb(part, by):
        last_local(part, by, mids[part].at[0]).wait()

        def arrive(index, carry):
            last_remote(part, by, index, mids[part].at[0]).wait_recv()
            return carry

        lax.fori_loop(1, 8, arrive, 0)
        keep(part, by).start()
        origin = (here[(part + 1) % 3] + SIDE - by) % SIDE
        rows = outs[part][:, origin].reshape(8 * PICK, WIDTHS[part])
        product = lax.dot_general(
            rows,
            weight[:, STARTS[part] : STARTS[part] + WIDTHS[part]],
            (((1,), (1,)), ((), ())),
            preferred_element_type=jnp.float32,
        )
        for block in range(8):
            for j in range(SIDE):
                coords = [None] * 3
                coords[part] = j
                coords[(part + 1) % 3] = origin
                coords[(part + 2) % 3] = block // 2
                group, owner = place(coords, block % 2)
                first = block * PICK + j * CAP
                device = group * 32 + owner
                total[device] = total[device] + product[first : first + CAP]

    total[...] = jnp.zeros_like(total)
    load_weight.wait()

    def push(index, carry):
        hidden_copy(index).start()
        return carry

    def onward(step, carry):
        @pl.when(step < SIDE)
        def _():
            turn = jnp.where(step < 3, 2 * step - 1, 2)
            for part in range(3):
                mid_copy(part, turn).wait()
            forward(turn, [mids[part].at[turn - 1] for part in range(3)])

        @pl.when(step < SIDE)
        def _():
            lax.fori_loop(43 * step - 42, jnp.minimum(43 * step + 1, 128), push, 0)

        for part in range(3):
            absorb(part, jnp.where(step < 2, 0, jnp.where(step < 4, 2 * step - 3, 2)))
        return carry

    lax.fori_loop(1, SIDE + 1, onward, 0)

    def settle(index, carry):
        hidden_copy(index).wait_send()
        return carry

    def collect(index, carry):
        hidden_copy(index).wait_recv()
        return carry

    own_hidden.wait()
    lax.fori_loop(1, 128, settle, 0)

    def pack(device, carry):
        rows = total[device]
        rows = jnp.concatenate([rows[:, :384], rows[:, 384:]], axis=0)
        answer[device] = rows.astype(jnp.bfloat16)
        return carry

    lax.fori_loop(0, 128, pack, 0)
    give = pltpu.make_async_copy(answer, answer_ref, local_sem.at[7])
    give.start()

    for part in range(3):

        def finish(i, carry, part=part):
            keep(part, i).wait()

            def body(index, inner):
                last_remote(part, i, index, mids[part].at[0]).wait_send()
                return inner

            return lax.fori_loop(1, 8, body, carry)

        lax.fori_loop(0, SIDE, finish, 0)
    lax.fori_loop(1, 128, collect, 0)
    give.wait()


def dispatch(*operands):
    vmem = pl.BlockSpec(memory_space=pltpu.VMEM)
    hbm = pl.BlockSpec(memory_space=pl.ANY)
    scratch = [
        pltpu.VMEM((768, 4096), jnp.bfloat16),
        pltpu.VMEM((128, CAP, 768), jnp.float32),
        pltpu.VMEM((128, 2 * CAP, 384), jnp.bfloat16),
    ]
    scratch += [pltpu.VMEM((8, SIDE, PICK, w), jnp.bfloat16) for w in WIDTHS]
    scratch += [pltpu.VMEM((512, w), jnp.bfloat16) for w in WIDTHS]
    scratch += [
        pltpu.VMEM((3, SIDE, 64, 128), jnp.float32),
        pltpu.VMEM((3, SIDE, 64, 128), jnp.float32),
        pltpu.VMEM((8 * PICK, 512), jnp.bfloat16),
    ]
    scratch += [pltpu.VMEM((SIDE, 8 * PICK, w), jnp.bfloat16) for w in WIDTHS]
    scratch += [pltpu.VMEM((SIDE - 1, 8 * PICK, w), jnp.bfloat16) for w in WIDTHS]
    scratch += [pltpu.SemaphoreType.DMA((9,))]
    scratch += [pltpu.SemaphoreType.DMA((3, SIDE)) for _ in range(7)]
    scratch += [pltpu.SemaphoreType.DMA((3, SIDE, 8)) for _ in range(2)]
    scratch += [pltpu.SemaphoreType.DMA((128,)) for _ in range(2)]
    shapes = [jax.ShapeDtypeStruct((8, SIDE, PICK, w), jnp.bfloat16) for w in WIDTHS]
    shapes += [jax.ShapeDtypeStruct((128, 2 * CAP, 384), jnp.bfloat16)] * 2
    return pl.pallas_call(
        dispatch_kernel,
        out_shape=shapes,
        in_specs=[vmem] * 7 + [hbm],
        out_specs=[hbm] * 5,
        scratch_shapes=scratch,
        compiler_params=pltpu.CompilerParams(
            collective_id=0, has_side_effects=True, vmem_limit_bytes=62 << 20
        ),
    )(*operands)


def arrange_kernel(got_ref, *out_refs):
    for part in range(3):

        def block_of(block, carry, part=part):
            pieces = []
            for j in range(SIDE):
                coords = [None] * 3
                coords[part] = j
                coords[(part + 1) % 3] = block % SIDE
                coords[(part + 2) % 3] = block // 8
                group, owner = place(coords, (block // SIDE) % 2)
                rows = got_ref[group * 32 + owner].astype(jnp.float32)
                pieces.append(jnp.concatenate([rows[:CAP], rows[CAP:]], axis=1))
            first = pl.multiple_of(block * PICK, PICK)
            out_refs[part][pl.ds(first, PICK)] = jnp.concatenate(pieces, axis=0).astype(
                jnp.bfloat16
            )
            return carry

        lax.fori_loop(0, 32, block_of, 0)


def arrange(got):
    vmem = pl.BlockSpec(memory_space=pltpu.VMEM)
    return pl.pallas_call(
        arrange_kernel,
        out_shape=[jax.ShapeDtypeStruct((1536, 768), jnp.bfloat16)] * 3,
        in_specs=[vmem],
        out_specs=[vmem] * 3,
        compiler_params=pltpu.CompilerParams(vmem_limit_bytes=24 << 20),
        cost_estimate=pl.CostEstimate(flops=0, bytes_accessed=10 << 20, transcendentals=0),
    )(got)


def restore_kernel(spot_ref, got_ref, out_ref, rows):
    def stage(block, carry):
        pieces = []
        for j in range(SIDE):
            piece = got_ref[block * SIDE + j].astype(jnp.float32)
            pieces.append(jnp.concatenate([piece[:CAP], piece[CAP:]], axis=1))
        first = pl.multiple_of(block * PICK, PICK)
        rows[pl.ds(first, PICK)] = jnp.concatenate(pieces, axis=0).astype(jnp.bfloat16)
        return carry

    lax.fori_loop(0, 32, stage, 0)
    for first in range(0, 1024, 256):
        place_of = lax.broadcasted_iota(jnp.int32, (256, 1536), 1)
        pick = jnp.where(spot_ref[first : first + 256] == place_of, 1.0, 0.0)
        out_ref[first : first + 256] = jnp.dot(
            pick.astype(jnp.bfloat16), rows[...], preferred_element_type=jnp.float32
        ).astype(jnp.bfloat16)


def restore(spot, got):
    vmem = pl.BlockSpec(memory_space=pltpu.VMEM)
    return pl.pallas_call(
        restore_kernel,
        out_shape=jax.ShapeDtypeStruct((1024, 768), jnp.bfloat16),
        in_specs=[vmem] * 2,
        out_specs=vmem,
        scratch_shapes=[pltpu.VMEM((1536, 768), jnp.bfloat16)],
        compiler_params=pltpu.CompilerParams(vmem_limit_bytes=24 << 20),
    )(spot, got)


def shards(hidden, out_grad, route_ids, gate_vals, rollout_ids, advantages, down_weight):
    slots = 1024
    named = jnp.sum(
        (route_ids[:, :, None] == jnp.arange(128, dtype=jnp.int32)).astype(jnp.bfloat16), axis=1
    )
    t = jnp.arange(128, dtype=jnp.int32)
    earlier = (t[:, None] > t[None, :]).astype(jnp.bfloat16)
    before = jnp.dot(earlier, named, preferred_element_type=jnp.float32)
    rank = jnp.sum(
        jnp.where(
            route_ids[:, :, None] == jnp.arange(128, dtype=jnp.int32), before[:, None, :], 0.0
        ),
        axis=2,
    ).astype(jnp.int32)
    spot = (route_ids * CAP + rank).reshape(slots)

    parts = dispatch(
        route_ids.T,
        gate_vals.T,
        rollout_ids,
        advantages,
        out_grad,
        spot[None, :],
        hidden.reshape(slots, 768),
        down_weight,
    )

    def exchange(rows):
        return lax.all_to_all(rows, ("grp", "ep"), split_axis=0, concat_axis=0, tiled=True)

    got_hidden = parts[4]
    returned = exchange(parts[3])
    grads = [
        lax.dot_general(
            rows,
            part.reshape(1536, width),
            (((0,), (0,)), ((), ())),
            preferred_element_type=jnp.float32,
        ).astype(jnp.bfloat16)
        for rows, part, width in zip(arrange(got_hidden), parts[:3], WIDTHS)
    ]
    weight_grad = jnp.concatenate(grads, axis=1)
    hidden_grad = restore(spot[:, None], returned)
    return hidden_grad.reshape(128, 8, 768), weight_grad[None]


def solution(mesh):
    wide = P(("grp", "ep"), None, None)
    flat = P(("grp", "ep"), None)
    return jax.shard_map(
        shards,
        mesh=mesh,
        in_specs=(wide, flat, flat, flat, flat, flat, wide),
        out_specs=(wide, wide),
        check_vma=False,
    )
```

```python
import jax
import jax.numpy as jnp
from jax import lax
from jax.experimental import pallas as pl
from jax.experimental.pallas import tpu as pltpu
from jax.sharding import PartitionSpec as P

MESH = pl.DeviceIdType.MESH
SIDE = 4
CAP = 12
STRIDE = 77
PICK = SIDE * CAP
WIDTHS = (1280, 1280, 1536)
STARTS = (0, 1280, 2560)


def position():
    group, owner = lax.axis_index("grp"), lax.axis_index("ep")
    core = group % 2
    z = (group // 2) * 2 + owner % 2
    x = (owner // 2) % 4
    y = owner // 8
    return (x, y, z), core


def place(coords, core):
    x, y, z = coords
    return ((z // 2) * 2 + core, y * 8 + x * 2 + z % 2)


def moved(coords, axis, by):
    new = list(coords)
    new[axis] = (coords[axis] + by) % SIDE
    return tuple(new)


def expert_rows(part):
    row = lax.broadcasted_iota(jnp.int32, (128, 128), 0)
    coords = [None] * 3
    coords[part % 3] = row // 32
    coords[(part + 1) % 3] = (row // 8) % 4
    coords[(part + 2) % 3] = (row // 2) % 4
    x, y, z = coords
    return ((z // 2) * 2 + row % 2) * 32 + y * 8 + x * 2 + z % 2


def dispatch_kernel(
    route_ref,
    gate_ref,
    rollout_ref,
    adv_ref,
    grad_ref,
    spot_ref,
    hidden_ref,
    weight_ref,
    kept0,
    kept1,
    kept2,
    answer_ref,
    got_hidden,
    weight,
    total,
    answer,
    out0,
    out1,
    out2,
    lines0,
    lines1,
    lines2,
    tables,
    got_tables,
    picks,
    send0,
    send1,
    send2,
    mid0,
    mid1,
    mid2,
    local_sem,
    keep_sem,
    line_send,
    line_recv,
    table_send,
    table_recv,
    mid_send,
    mid_recv,
    last_send,
    last_recv,
    hidden_send,
    hidden_recv,
):
    outs, lines = (out0, out1, out2), (lines0, lines1, lines2)
    kept = (kept0, kept1, kept2)
    sends, mids = (send0, send1, send2), (mid0, mid1, mid2)
    here, core = position()

    barrier = pltpu.get_barrier_semaphore()
    me = lax.axis_index("grp") * 32 + lax.axis_index("ep")

    def other(index):
        shift = (index * STRIDE) & 127
        x, y, z = here
        x, y, z = (x + (shift >> 1)) & 3, (y + (shift >> 3)) & 3, (z + (shift >> 5)) & 3
        return ((z & 2) + ((core + shift) & 1), y * 8 + x * 2 + (z & 1))

    def greet(index, carry):
        pl.semaphore_signal(barrier, inc=1, device_id=other(index), device_id_type=MESH)
        return carry

    lax.fori_loop(1, 128, greet, 0)
    pl.semaphore_wait(barrier, 127)

    def line_copy(part, by):
        there = place(moved(here, part, by), core)
        return pltpu.make_async_remote_copy(
            src_ref=grad_ref.at[:, pl.ds(STARTS[part], WIDTHS[part])],
            dst_ref=lines[part].at[pl.ds(pl.multiple_of(here[part] * 128, 128), 128)],
            send_sem=line_send.at[part, by],
            recv_sem=line_recv.at[part, by],
            device_id=there,
            device_id_type=MESH,
        )

    def own_line(part):
        return pltpu.make_async_copy(
            grad_ref.at[:, pl.ds(STARTS[part], WIDTHS[part])],
            lines[part].at[pl.ds(pl.multiple_of(here[part] * 128, 128), 128)],
            local_sem.at[part],
        )

    def table_copy(part, by):
        target = moved(here, part, by)
        return pltpu.make_async_remote_copy(
            src_ref=tables.at[part, target[part]],
            dst_ref=got_tables.at[part, here[part]],
            send_sem=table_send.at[part, by],
            recv_sem=table_recv.at[part, by],
            device_id=place(target, core),
            device_id_type=MESH,
        )

    def own_table(part):
        return pltpu.make_async_copy(
            tables.at[part, here[part]], got_tables.at[part, here[part]], local_sem.at[3 + part]
        )

    for by in (1, 3, 2):
        for part in range(3):
            line_copy(part, by).start()
    for part in range(3):
        own_line(part).start()
    load_weight = pltpu.make_async_copy(weight_ref.at[0], weight, local_sem.at[6])
    load_weight.start()

    rollout = rollout_ref[...]
    token_weight = jnp.zeros((1, 128), jnp.float32)
    for i in range(4):
        hit = (rollout == i).astype(jnp.float32)
        count = jnp.sum(hit, axis=1, keepdims=True)
        token_weight = token_weight + hit * (adv_ref[:, i : i + 1] * 32.0 / count)
    scale = gate_ref[...] * token_weight
    route = route_ref[...]
    sooner = (
        lax.broadcasted_iota(jnp.int32, (128, 128), 0)
        < lax.broadcasted_iota(jnp.int32, (128, 128), 1)
    ).astype(jnp.bfloat16)
    for part in range(3):
        expert = expert_rows(part)
        named = jnp.zeros((128, 128), jnp.float32)
        held = jnp.zeros((128, 128), jnp.float32)
        for k in range(8):
            match = route[k : k + 1, :] == expert
            named = named + jnp.where(match, 1.0, 0.0)
            held = held + jnp.where(match, scale[k : k + 1, :], 0.0)
        rank = jnp.dot(named.astype(jnp.bfloat16), sooner, preferred_element_type=jnp.float32)
        rank = jnp.where(named > 0.5, rank, -1.0)
        for i in range(SIDE):
            tables[part, i, 0:32] = rank[32 * i : 32 * i + 32]
            tables[part, i, 32:64] = held[32 * i : 32 * i + 32]
    for by in (1, 3, 2):
        for part in range(3):
            table_copy(part, by).start()
    for part in range(3):
        own_table(part).start()

    def hidden_copy(index):
        group, owner = other(index)
        return pltpu.make_async_remote_copy(
            src_ref=answer.at[group * 32 + owner],
            dst_ref=got_hidden.at[me],
            send_sem=hidden_send.at[index],
            recv_sem=hidden_recv.at[index],
            device_id=(group, owner),
            device_id_type=MESH,
        )

    own_hidden = pltpu.make_async_copy(answer.at[me], got_hidden.at[me], local_sem.at[8])

    def gather(block, carry):
        wanted_spot = lax.broadcasted_iota(jnp.int32, (384, 1024), 0) + block * 384
        pick = jnp.where(wanted_spot == spot_ref[...], 1.0, 0.0).astype(jnp.bfloat16)
        found = jnp.dot(pick, hidden_ref[...], preferred_element_type=jnp.float32)
        for i in range(32):
            rows = found[i * CAP : i * CAP + CAP]
            rows = jnp.concatenate([rows[:, :384], rows[:, 384:]], axis=0)
            answer[block * 32 + i] = rows.astype(jnp.bfloat16)
        return carry

    lax.fori_loop(0, 4, gather, 0)
    own_hidden.start()

    def mid_copy(part, by):
        return pltpu.make_async_remote_copy(
            src_ref=sends[part].at[by],
            dst_ref=mids[part].at[by - 1],
            send_sem=mid_send.at[part, by],
            recv_sem=mid_recv.at[part, by],
            device_id=place(moved(here, (part + 1) % 3, by), core),
            device_id_type=MESH,
        )

    def last_copy(part, by, step, flip, source):
        second, third = (part + 1) % 3, (part + 2) % 3
        target = moved(here, third, step)
        there_core = (core + flip) % 2
        rows = pl.ds(pl.multiple_of((target[third] * 2 + there_core) * PICK, PICK), PICK)
        origin = (here[second] + SIDE - by) % SIDE
        block = here[third] * 2 + core
        return source.at[rows], outs[part].at[block, origin], target, there_core

    def last_remote(part, by, index, source):
        step, flip = index // 2, index % 2
        src, dst, target, there_core = last_copy(part, by, step, flip, source)
        return pltpu.make_async_remote_copy(
            src_ref=src,
            dst_ref=dst,
            send_sem=last_send.at[part, by, index],
            recv_sem=last_recv.at[part, by, index],
            device_id=place(target, there_core),
            device_id_type=MESH,
        )

    def last_local(part, by, source):
        src, dst, _, _ = last_copy(part, by, 0, 0, source)
        return pltpu.make_async_copy(src, dst, last_recv.at[part, by, 0])

    def forward(by, sources):
        for part in range(3):
            last_local(part, by, sources[part]).start()

        def body(index, carry):
            for part in range(3):
                last_remote(part, by, (3 * index) & 7, sources[part]).start()
            return carry

        lax.fori_loop(1, 8, body, 0)

    row = lax.broadcasted_iota(jnp.int32, (PICK, 512), 0)
    lane = lax.broadcasted_iota(jnp.int32, (PICK, 512), 1)
    wanted = jnp.where(lane // 128 == row // CAP, row % CAP, -7).astype(jnp.float32)

    for part in range(3):
        own_line(part).wait()
        own_table(part).wait()
        for by in (1, 3, 2):
            line_copy(part, by).wait()
            table_copy(part, by).wait()

    def select(i, carry):
        by = jnp.where(i < 2, 2 * i + 1, 6 - 2 * i)
        for part in range(3):
            target = (here[(part + 1) % 3] + by) % SIDE
            first = pl.multiple_of(target * 8, 8)
            ranks = jnp.concatenate(
                [got_tables[part, s, pl.ds(first, 8), :] for s in range(SIDE)], axis=1
            )
            helds = jnp.concatenate(
                [got_tables[part, s, pl.ds(first + 32, 8), :] for s in range(SIDE)], axis=1
            )
            scales = []
            for j in range(8):
                hit = ranks[j : j + 1, :] == wanted
                picks[pl.ds(j * PICK, PICK), :] = jnp.where(hit, 1.0, 0.0).astype(jnp.bfloat16)
                scales.append(
                    jnp.sum(jnp.where(hit, helds[j : j + 1, :], 0.0), axis=1, keepdims=True)
                )
            factor = jnp.concatenate(scales, axis=0)
            for start in range(0, WIDTHS[part], 256):
                found = jnp.dot(
                    picks[...],
                    lines[part][:, start : start + 256],
                    preferred_element_type=jnp.float32,
                )
                sends[part][by, :, start : start + 256] = (found * factor).astype(jnp.bfloat16)

            @pl.when(by > 0)
            def _():
                mid_copy(part, by).start()

        return carry

    lax.fori_loop(0, SIDE, select, 0)
    forward(0, [sends[part].at[0] for part in range(3)])

    def keep(part, by):
        origin = (here[(part + 1) % 3] + SIDE - by) % SIDE
        return pltpu.make_async_copy(
            outs[part].at[:, origin], kept[part].at[:, origin], keep_sem.at[part, by]
        )

    def absorb(part, by):
        last_local(part, by, mids[part].at[0]).wait()

        def arrive(index, carry):
            last_remote(part, by, index, mids[part].at[0]).wait_recv()
            return carry

        lax.fori_loop(1, 8, arrive, 0)
        keep(part, by).start()
        origin = (here[(part + 1) % 3] + SIDE - by) % SIDE
        rows = outs[part][:, origin].reshape(8 * PICK, WIDTHS[part])
        product = lax.dot_general(
            rows,
            weight[:, STARTS[part] : STARTS[part] + WIDTHS[part]],
            (((1,), (1,)), ((), ())),
            preferred_element_type=jnp.float32,
        )
        for block in range(8):
            for j in range(SIDE):
                coords = [None] * 3
                coords[part] = j
                coords[(part + 1) % 3] = origin
                coords[(part + 2) % 3] = block // 2
                group, owner = place(coords, block % 2)
                first = block * PICK + j * CAP
                device = group * 32 + owner
                total[device] = total[device] + product[first : first + CAP]

    total[...] = jnp.zeros_like(total)
    load_weight.wait()

    def push(index, carry):
        hidden_copy(index).start()
        return carry

    def onward(step, carry):
        @pl.when(step < SIDE)
        def _():
            turn = jnp.where(step < 3, 2 * step - 1, 2)
            for part in range(3):
                mid_copy(part, turn).wait()
            forward(turn, [mids[part].at[turn - 1] for part in range(3)])

        @pl.when(step < SIDE)
        def _():
            lax.fori_loop(43 * step - 42, jnp.minimum(43 * step + 1, 128), push, 0)

        for part in range(3):
            absorb(part, jnp.where(step < 2, 0, jnp.where(step < 4, 2 * step - 3, 2)))
        return carry

    lax.fori_loop(1, SIDE + 1, onward, 0)

    def settle(index, carry):
        hidden_copy(index).wait_send()
        return carry

    def collect(index, carry):
        hidden_copy(index).wait_recv()
        return carry

    own_hidden.wait()
    lax.fori_loop(1, 128, settle, 0)

    def pack(device, carry):
        rows = total[device]
        rows = jnp.concatenate([rows[:, :384], rows[:, 384:]], axis=0)
        answer[device] = rows.astype(jnp.bfloat16)
        return carry

    lax.fori_loop(0, 128, pack, 0)
    give = pltpu.make_async_copy(answer, answer_ref, local_sem.at[7])
    give.start()

    for part in range(3):

        def finish(i, carry, part=part):
            keep(part, i).wait()

            def body(index, inner):
                last_remote(part, i, index, mids[part].at[0]).wait_send()
                return inner

            return lax.fori_loop(1, 8, body, carry)

        lax.fori_loop(0, SIDE, finish, 0)
    lax.fori_loop(1, 128, collect, 0)
    give.wait()


def dispatch(*operands):
    vmem = pl.BlockSpec(memory_space=pltpu.VMEM)
    hbm = pl.BlockSpec(memory_space=pl.ANY)
    scratch = [
        pltpu.VMEM((768, 4096), jnp.bfloat16),
        pltpu.VMEM((128, CAP, 768), jnp.float32),
        pltpu.VMEM((128, 2 * CAP, 384), jnp.bfloat16),
    ]
    scratch += [pltpu.VMEM((8, SIDE, PICK, w), jnp.bfloat16) for w in WIDTHS]
    scratch += [pltpu.VMEM((512, w), jnp.bfloat16) for w in WIDTHS]
    scratch += [
        pltpu.VMEM((3, SIDE, 64, 128), jnp.float32),
        pltpu.VMEM((3, SIDE, 64, 128), jnp.float32),
        pltpu.VMEM((8 * PICK, 512), jnp.bfloat16),
    ]
    scratch += [pltpu.VMEM((SIDE, 8 * PICK, w), jnp.bfloat16) for w in WIDTHS]
    scratch += [pltpu.VMEM((SIDE - 1, 8 * PICK, w), jnp.bfloat16) for w in WIDTHS]
    scratch += [pltpu.SemaphoreType.DMA((9,))]
    scratch += [pltpu.SemaphoreType.DMA((3, SIDE)) for _ in range(7)]
    scratch += [pltpu.SemaphoreType.DMA((3, SIDE, 8)) for _ in range(2)]
    scratch += [pltpu.SemaphoreType.DMA((128,)) for _ in range(2)]
    shapes = [jax.ShapeDtypeStruct((8, SIDE, PICK, w), jnp.bfloat16) for w in WIDTHS]
    shapes += [jax.ShapeDtypeStruct((128, 2 * CAP, 384), jnp.bfloat16)] * 2
    return pl.pallas_call(
        dispatch_kernel,
        out_shape=shapes,
        in_specs=[vmem] * 7 + [hbm],
        out_specs=[hbm] * 5,
        scratch_shapes=scratch,
        compiler_params=pltpu.CompilerParams(
            collective_id=0, has_side_effects=True, vmem_limit_bytes=62 << 20
        ),
    )(*operands)


TILE = 256


def weight_grad_kernel(got_ref, scaled0, scaled1, scaled2, out_ref, rows, turned):
    step = pl.program_id(0)
    for part, scaled in enumerate((scaled0, scaled1, scaled2)):
        first_step = STARTS[part] // TILE
        last_step = first_step + WIDTHS[part] // TILE

        def block_of(block, carry, part=part):
            pieces = []
            for j in range(SIDE):
                coords = [None] * 3
                coords[part] = j
                coords[(part + 1) % 3] = block % SIDE
                coords[(part + 2) % 3] = block // 8
                group, owner = place(coords, (block // SIDE) % 2)
                piece = got_ref[group * 32 + owner].astype(jnp.float32)
                pieces.append(jnp.concatenate([piece[:CAP], piece[CAP:]], axis=1))
            first = pl.multiple_of(block * PICK, PICK)
            rows[pl.ds(first, PICK)] = jnp.concatenate(pieces, axis=0)
            return carry

        @pl.when(step == first_step)
        def _():
            lax.fori_loop(0, 32, block_of, 0)
            for first in range(0, 1536, 128):
                turned[:, first : first + 128] = rows[first : first + 128].T.astype(jnp.bfloat16)

        @pl.when((step >= first_step) & (step < last_step))
        def _():
            out_ref[...] = jnp.dot(
                turned[...], scaled[...], preferred_element_type=jnp.float32
            ).astype(jnp.bfloat16)


def weight_gradient(got, parts):
    def columns(part):
        first, count = STARTS[part] // TILE, WIDTHS[part] // TILE
        return pl.BlockSpec((1536, TILE), lambda i: (0, jnp.clip(i - first, 0, count - 1)))

    return pl.pallas_call(
        weight_grad_kernel,
        grid=(4096 // TILE,),
        out_shape=jax.ShapeDtypeStruct((768, 4096), jnp.bfloat16),
        in_specs=[pl.BlockSpec((128, 2 * CAP, 384), lambda i: (0, 0, 0))]
        + [columns(part) for part in range(3)],
        out_specs=pl.BlockSpec((768, TILE), lambda i: (0, i)),
        scratch_shapes=[
            pltpu.VMEM((1536, 768), jnp.float32),
            pltpu.VMEM((768, 1536), jnp.bfloat16),
        ],
        compiler_params=pltpu.CompilerParams(vmem_limit_bytes=40 << 20),
        cost_estimate=pl.CostEstimate(
            flops=2 * 1536 * 768 * 4096, bytes_accessed=24 << 20, transcendentals=0
        ),
    )(got, *[rows.reshape(1536, width) for rows, width in zip(parts, WIDTHS)])


def restore_kernel(spot_ref, got_ref, out_ref, rows):
    def stage(block, carry):
        pieces = []
        for j in range(SIDE):
            piece = got_ref[block * SIDE + j].astype(jnp.float32)
            pieces.append(jnp.concatenate([piece[:CAP], piece[CAP:]], axis=1))
        first = pl.multiple_of(block * PICK, PICK)
        rows[pl.ds(first, PICK)] = jnp.concatenate(pieces, axis=0).astype(jnp.bfloat16)
        return carry

    lax.fori_loop(0, 32, stage, 0)
    for first in range(0, 1024, 256):
        place_of = lax.broadcasted_iota(jnp.int32, (256, 1536), 1)
        pick = jnp.where(spot_ref[first : first + 256] == place_of, 1.0, 0.0)
        out_ref[first : first + 256] = jnp.dot(
            pick.astype(jnp.bfloat16), rows[...], preferred_element_type=jnp.float32
        ).astype(jnp.bfloat16)


def restore(spot, got):
    vmem = pl.BlockSpec(memory_space=pltpu.VMEM)
    return pl.pallas_call(
        restore_kernel,
        out_shape=jax.ShapeDtypeStruct((1024, 768), jnp.bfloat16),
        in_specs=[vmem] * 2,
        out_specs=vmem,
        scratch_shapes=[pltpu.VMEM((1536, 768), jnp.bfloat16)],
        compiler_params=pltpu.CompilerParams(vmem_limit_bytes=24 << 20),
    )(spot, got)


def shards(hidden, out_grad, route_ids, gate_vals, rollout_ids, advantages, down_weight):
    slots = 1024
    named = jnp.sum(
        (route_ids[:, :, None] == jnp.arange(128, dtype=jnp.int32)).astype(jnp.bfloat16), axis=1
    )
    t = jnp.arange(128, dtype=jnp.int32)
    earlier = (t[:, None] > t[None, :]).astype(jnp.bfloat16)
    before = jnp.dot(earlier, named, preferred_element_type=jnp.float32)
    rank = jnp.sum(
        jnp.where(
            route_ids[:, :, None] == jnp.arange(128, dtype=jnp.int32), before[:, None, :], 0.0
        ),
        axis=2,
    ).astype(jnp.int32)
    spot = (route_ids * CAP + rank).reshape(slots)

    parts = dispatch(
        route_ids.T,
        gate_vals.T,
        rollout_ids,
        advantages,
        out_grad,
        spot[None, :],
        hidden.reshape(slots, 768),
        down_weight,
    )

    def exchange(rows):
        return lax.all_to_all(rows, ("grp", "ep"), split_axis=0, concat_axis=0, tiled=True)

    got_hidden = parts[4]
    returned = exchange(parts[3])
    weight_grad = weight_gradient(got_hidden, parts[:3])
    hidden_grad = restore(spot[:, None], returned)
    return hidden_grad.reshape(128, 8, 768), weight_grad[None]


def solution(mesh):
    wide = P(("grp", "ep"), None, None)
    flat = P(("grp", "ep"), None)
    return jax.shard_map(
        shards,
        mesh=mesh,
        in_specs=(wide, flat, flat, flat, flat, flat, wide),
        out_specs=(wide, wide),
        check_vma=False,
    )
```

```python
import jax
import jax.numpy as jnp
from jax import lax
from jax.experimental import pallas as pl
from jax.experimental.pallas import tpu as pltpu
from jax.sharding import PartitionSpec as P

MESH = pl.DeviceIdType.MESH
SIDE = 4
CAP = 12
STRIDE = 77
PICK = SIDE * CAP
WIDTHS = (1280, 1280, 1536)
STARTS = (0, 1280, 2560)


def position():
    group, owner = lax.axis_index("grp"), lax.axis_index("ep")
    core = group % 2
    z = (group // 2) * 2 + owner % 2
    x = (owner // 2) % 4
    y = owner // 8
    return (x, y, z), core


def place(coords, core):
    x, y, z = coords
    return ((z // 2) * 2 + core, y * 8 + x * 2 + z % 2)


def moved(coords, axis, by):
    new = list(coords)
    new[axis] = (coords[axis] + by) % SIDE
    return tuple(new)


def expert_rows(part):
    row = lax.broadcasted_iota(jnp.int32, (128, 128), 0)
    coords = [None] * 3
    coords[part % 3] = row // 32
    coords[(part + 1) % 3] = (row // 8) % 4
    coords[(part + 2) % 3] = (row // 2) % 4
    x, y, z = coords
    return ((z // 2) * 2 + row % 2) * 32 + y * 8 + x * 2 + z % 2


def dispatch_kernel(
    route_ref,
    gate_ref,
    rollout_ref,
    adv_ref,
    grad_ref,
    spot_ref,
    hidden_ref,
    weight_ref,
    kept0,
    kept1,
    kept2,
    answer_ref,
    got_hidden,
    weight,
    total,
    answer,
    out0,
    out1,
    out2,
    lines0,
    lines1,
    lines2,
    tables,
    got_tables,
    picks,
    send0,
    send1,
    send2,
    mid0,
    mid1,
    mid2,
    local_sem,
    keep_sem,
    line_send,
    line_recv,
    table_send,
    table_recv,
    mid_send,
    mid_recv,
    last_send,
    last_recv,
    hidden_send,
    hidden_recv,
):
    outs, lines = (out0, out1, out2), (lines0, lines1, lines2)
    kept = (kept0, kept1, kept2)
    sends, mids = (send0, send1, send2), (mid0, mid1, mid2)
    here, core = position()

    barrier = pltpu.get_barrier_semaphore()
    me = lax.axis_index("grp") * 32 + lax.axis_index("ep")

    def other(index):
        shift = (index * STRIDE) & 127
        x, y, z = here
        x, y, z = (x + (shift >> 1)) & 3, (y + (shift >> 3)) & 3, (z + (shift >> 5)) & 3
        return ((z & 2) + ((core + shift) & 1), y * 8 + x * 2 + (z & 1))

    def greet(index, carry):
        pl.semaphore_signal(barrier, inc=1, device_id=other(index), device_id_type=MESH)
        return carry

    lax.fori_loop(1, 128, greet, 0)
    pl.semaphore_wait(barrier, 127)

    def line_copy(part, by):
        there = place(moved(here, part, by), core)
        return pltpu.make_async_remote_copy(
            src_ref=grad_ref.at[:, pl.ds(STARTS[part], WIDTHS[part])],
            dst_ref=lines[part].at[pl.ds(pl.multiple_of(here[part] * 128, 128), 128)],
            send_sem=line_send.at[part, by],
            recv_sem=line_recv.at[part, by],
            device_id=there,
            device_id_type=MESH,
        )

    def own_line(part):
        return pltpu.make_async_copy(
            grad_ref.at[:, pl.ds(STARTS[part], WIDTHS[part])],
            lines[part].at[pl.ds(pl.multiple_of(here[part] * 128, 128), 128)],
            local_sem.at[part],
        )

    def table_copy(part, by):
        target = moved(here, part, by)
        return pltpu.make_async_remote_copy(
            src_ref=tables.at[part, target[part]],
            dst_ref=got_tables.at[part, here[part]],
            send_sem=table_send.at[part, by],
            recv_sem=table_recv.at[part, by],
            device_id=place(target, core),
            device_id_type=MESH,
        )

    def own_table(part):
        return pltpu.make_async_copy(
            tables.at[part, here[part]], got_tables.at[part, here[part]], local_sem.at[3 + part]
        )

    for by in (1, 3, 2):
        for part in range(3):
            line_copy(part, by).start()
    for part in range(3):
        own_line(part).start()
    load_weight = pltpu.make_async_copy(weight_ref.at[0], weight, local_sem.at[6])
    load_weight.start()

    rollout = rollout_ref[...]
    token_weight = jnp.zeros((1, 128), jnp.float32)
    for i in range(4):
        hit = (rollout == i).astype(jnp.float32)
        count = jnp.sum(hit, axis=1, keepdims=True)
        token_weight = token_weight + hit * (adv_ref[:, i : i + 1] * 32.0 / count)
    scale = gate_ref[...] * token_weight
    route = route_ref[...]
    sooner = (
        lax.broadcasted_iota(jnp.int32, (128, 128), 0)
        < lax.broadcasted_iota(jnp.int32, (128, 128), 1)
    ).astype(jnp.bfloat16)
    for part in range(3):
        expert = expert_rows(part)
        named = jnp.zeros((128, 128), jnp.float32)
        held = jnp.zeros((128, 128), jnp.float32)
        for k in range(8):
            match = route[k : k + 1, :] == expert
            named = named + jnp.where(match, 1.0, 0.0)
            held = held + jnp.where(match, scale[k : k + 1, :], 0.0)
        rank = jnp.dot(named.astype(jnp.bfloat16), sooner, preferred_element_type=jnp.float32)
        rank = jnp.where(named > 0.5, rank, -1.0)
        for i in range(SIDE):
            tables[part, i, 0:32] = rank[32 * i : 32 * i + 32]
            tables[part, i, 32:64] = held[32 * i : 32 * i + 32]
    for by in (1, 3, 2):
        for part in range(3):
            table_copy(part, by).start()
    for part in range(3):
        own_table(part).start()

    def hidden_copy(index):
        group, owner = other(index)
        return pltpu.make_async_remote_copy(
            src_ref=answer.at[group * 32 + owner],
            dst_ref=got_hidden.at[me],
            send_sem=hidden_send.at[index],
            recv_sem=hidden_recv.at[index],
            device_id=(group, owner),
            device_id_type=MESH,
        )

    own_hidden = pltpu.make_async_copy(answer.at[me], got_hidden.at[me], local_sem.at[8])

    def gather(block, carry):
        wanted_spot = lax.broadcasted_iota(jnp.int32, (384, 1024), 0) + block * 384
        pick = jnp.where(wanted_spot == spot_ref[...], 1.0, 0.0).astype(jnp.bfloat16)
        found = jnp.dot(pick, hidden_ref[...], preferred_element_type=jnp.float32)
        for i in range(32):
            rows = found[i * CAP : i * CAP + CAP]
            rows = jnp.concatenate([rows[:, :384], rows[:, 384:]], axis=0)
            answer[block * 32 + i] = rows.astype(jnp.bfloat16)
        return carry

    lax.fori_loop(0, 4, gather, 0)
    own_hidden.start()

    def mid_copy(part, by):
        return pltpu.make_async_remote_copy(
            src_ref=sends[part].at[by],
            dst_ref=mids[part].at[by - 1],
            send_sem=mid_send.at[part, by],
            recv_sem=mid_recv.at[part, by],
            device_id=place(moved(here, (part + 1) % 3, by), core),
            device_id_type=MESH,
        )

    def last_copy(part, by, step, flip, source):
        second, third = (part + 1) % 3, (part + 2) % 3
        target = moved(here, third, step)
        there_core = (core + flip) % 2
        rows = pl.ds(pl.multiple_of((target[third] * 2 + there_core) * PICK, PICK), PICK)
        origin = (here[second] + SIDE - by) % SIDE
        block = here[third] * 2 + core
        return source.at[rows], outs[part].at[block, origin], target, there_core

    def last_remote(part, by, index, source):
        step, flip = index // 2, index % 2
        src, dst, target, there_core = last_copy(part, by, step, flip, source)
        return pltpu.make_async_remote_copy(
            src_ref=src,
            dst_ref=dst,
            send_sem=last_send.at[part, by, index],
            recv_sem=last_recv.at[part, by, index],
            device_id=place(target, there_core),
            device_id_type=MESH,
        )

    def last_local(part, by, source):
        src, dst, _, _ = last_copy(part, by, 0, 0, source)
        return pltpu.make_async_copy(src, dst, last_recv.at[part, by, 0])

    def forward(by, sources):
        for part in range(3):
            last_local(part, by, sources[part]).start()

        def body(index, carry):
            for part in range(3):
                last_remote(part, by, (3 * index) & 7, sources[part]).start()
            return carry

        lax.fori_loop(1, 8, body, 0)

    row = lax.broadcasted_iota(jnp.int32, (PICK, 512), 0)
    lane = lax.broadcasted_iota(jnp.int32, (PICK, 512), 1)
    wanted = jnp.where(lane // 128 == row // CAP, row % CAP, -7).astype(jnp.float32)

    for part in range(3):
        own_line(part).wait()
        own_table(part).wait()
        for by in (1, 3, 2):
            line_copy(part, by).wait()
            table_copy(part, by).wait()

    def select(i, carry):
        by = jnp.where(i < 2, 2 * i + 1, 6 - 2 * i)
        for part in range(3):
            target = (here[(part + 1) % 3] + by) % SIDE
            first = pl.multiple_of(target * 8, 8)
            ranks = jnp.concatenate(
                [got_tables[part, s, pl.ds(first, 8), :] for s in range(SIDE)], axis=1
            )
            helds = jnp.concatenate(
                [got_tables[part, s, pl.ds(first + 32, 8), :] for s in range(SIDE)], axis=1
            )
            scales = []
            for j in range(8):
                hit = ranks[j : j + 1, :] == wanted
                picks[pl.ds(j * PICK, PICK), :] = jnp.where(hit, 1.0, 0.0).astype(jnp.bfloat16)
                scales.append(
                    jnp.sum(jnp.where(hit, helds[j : j + 1, :], 0.0), axis=1, keepdims=True)
                )
            factor = jnp.concatenate(scales, axis=0)
            for start in range(0, WIDTHS[part], 256):
                found = jnp.dot(
                    picks[...],
                    lines[part][:, start : start + 256],
                    preferred_element_type=jnp.float32,
                )
                sends[part][by, :, start : start + 256] = (found * factor).astype(jnp.bfloat16)

            @pl.when(by > 0)
            def _():
                mid_copy(part, by).start()

        return carry

    lax.fori_loop(0, SIDE, select, 0)
    forward(0, [sends[part].at[0] for part in range(3)])

    def keep(part, by):
        origin = (here[(part + 1) % 3] + SIDE - by) % SIDE
        return pltpu.make_async_copy(
            outs[part].at[:, origin], kept[part].at[:, origin], keep_sem.at[part, by]
        )

    def absorb(part, by):
        last_local(part, by, mids[part].at[0]).wait()

        def arrive(index, carry):
            last_remote(part, by, index, mids[part].at[0]).wait_recv()
            return carry

        lax.fori_loop(1, 8, arrive, 0)
        keep(part, by).start()
        origin = (here[(part + 1) % 3] + SIDE - by) % SIDE
        rows = outs[part][:, origin].reshape(8 * PICK, WIDTHS[part])
        product = lax.dot_general(
            rows,
            weight[:, STARTS[part] : STARTS[part] + WIDTHS[part]],
            (((1,), (1,)), ((), ())),
            preferred_element_type=jnp.float32,
        )
        for block in range(8):
            for j in range(SIDE):
                coords = [None] * 3
                coords[part] = j
                coords[(part + 1) % 3] = origin
                coords[(part + 2) % 3] = block // 2
                group, owner = place(coords, block % 2)
                first = block * PICK + j * CAP
                device = group * 32 + owner
                total[device] = total[device] + product[first : first + CAP]

    total[...] = jnp.zeros_like(total)
    load_weight.wait()

    def push(index, carry):
        hidden_copy(index).start()
        return carry

    def onward(step, carry):
        turn = jnp.where(step < 3, 2 * step - 1, 2)
        for part in range(3):
            mid_copy(part, turn).wait()
        forward(turn, [mids[part].at[turn - 1] for part in range(3)])
        lax.fori_loop(43 * step - 42, jnp.minimum(43 * step + 1, 128), push, 0)
        return carry

    def gain(step, carry):
        for part in range(3):
            absorb(part, jnp.where(step < 2, 0, jnp.where(step < 4, 2 * step - 3, 2)))
        return carry

    lax.fori_loop(1, SIDE, onward, 0)
    lax.fori_loop(1, SIDE + 1, gain, 0)

    def settle(index, carry):
        hidden_copy(index).wait_send()
        return carry

    def collect(index, carry):
        hidden_copy(index).wait_recv()
        return carry

    own_hidden.wait()
    lax.fori_loop(1, 128, settle, 0)

    def pack(device, carry):
        rows = total[device]
        rows = jnp.concatenate([rows[:, :384], rows[:, 384:]], axis=0)
        answer[device] = rows.astype(jnp.bfloat16)
        return carry

    lax.fori_loop(0, 128, pack, 0)
    give = pltpu.make_async_copy(answer, answer_ref, local_sem.at[7])
    give.start()

    for part in range(3):

        def finish(i, carry, part=part):
            keep(part, i).wait()

            def body(index, inner):
                last_remote(part, i, index, mids[part].at[0]).wait_send()
                return inner

            return lax.fori_loop(1, 8, body, carry)

        lax.fori_loop(0, SIDE, finish, 0)
    lax.fori_loop(1, 128, collect, 0)
    give.wait()


def dispatch(*operands):
    vmem = pl.BlockSpec(memory_space=pltpu.VMEM)
    hbm = pl.BlockSpec(memory_space=pl.ANY)
    scratch = [
        pltpu.VMEM((768, 4096), jnp.bfloat16),
        pltpu.VMEM((128, CAP, 768), jnp.float32),
        pltpu.VMEM((128, 2 * CAP, 384), jnp.bfloat16),
    ]
    scratch += [pltpu.VMEM((8, SIDE, PICK, w), jnp.bfloat16) for w in WIDTHS]
    scratch += [pltpu.VMEM((512, w), jnp.bfloat16) for w in WIDTHS]
    scratch += [
        pltpu.VMEM((3, SIDE, 64, 128), jnp.float32),
        pltpu.VMEM((3, SIDE, 64, 128), jnp.float32),
        pltpu.VMEM((8 * PICK, 512), jnp.bfloat16),
    ]
    scratch += [pltpu.VMEM((SIDE, 8 * PICK, w), jnp.bfloat16) for w in WIDTHS]
    scratch += [pltpu.VMEM((SIDE - 1, 8 * PICK, w), jnp.bfloat16) for w in WIDTHS]
    scratch += [pltpu.SemaphoreType.DMA((9,))]
    scratch += [pltpu.SemaphoreType.DMA((3, SIDE)) for _ in range(7)]
    scratch += [pltpu.SemaphoreType.DMA((3, SIDE, 8)) for _ in range(2)]
    scratch += [pltpu.SemaphoreType.DMA((128,)) for _ in range(2)]
    shapes = [jax.ShapeDtypeStruct((8, SIDE, PICK, w), jnp.bfloat16) for w in WIDTHS]
    shapes += [jax.ShapeDtypeStruct((128, 2 * CAP, 384), jnp.bfloat16)] * 2
    return pl.pallas_call(
        dispatch_kernel,
        out_shape=shapes,
        in_specs=[vmem] * 7 + [hbm],
        out_specs=[hbm] * 5,
        scratch_shapes=scratch,
        compiler_params=pltpu.CompilerParams(
            collective_id=0, has_side_effects=True, vmem_limit_bytes=62 << 20
        ),
    )(*operands)


TILE = 256


def weight_grad_kernel(got_ref, scaled0, scaled1, scaled2, out_ref, rows, turned):
    step = pl.program_id(0)
    for part, scaled in enumerate((scaled0, scaled1, scaled2)):
        first_step = STARTS[part] // TILE
        last_step = first_step + WIDTHS[part] // TILE

        def block_of(block, carry, part=part):
            pieces = []
            for j in range(SIDE):
                coords = [None] * 3
                coords[part] = j
                coords[(part + 1) % 3] = block % SIDE
                coords[(part + 2) % 3] = block // 8
                group, owner = place(coords, (block // SIDE) % 2)
                piece = got_ref[group * 32 + owner].astype(jnp.float32)
                pieces.append(jnp.concatenate([piece[:CAP], piece[CAP:]], axis=1))
            first = pl.multiple_of(block * PICK, PICK)
            rows[pl.ds(first, PICK)] = jnp.concatenate(pieces, axis=0)
            return carry

        @pl.when(step == first_step)
        def _():
            lax.fori_loop(0, 32, block_of, 0)
            for first in range(0, 1536, 128):
                turned[:, first : first + 128] = rows[first : first + 128].T.astype(jnp.bfloat16)

        @pl.when((step >= first_step) & (step < last_step))
        def _():
            out_ref[...] = jnp.dot(
                turned[...], scaled[...], preferred_element_type=jnp.float32
            ).astype(jnp.bfloat16)


def weight_gradient(got, parts):
    def columns(part):
        first, count = STARTS[part] // TILE, WIDTHS[part] // TILE
        return pl.BlockSpec((1536, TILE), lambda i: (0, jnp.clip(i - first, 0, count - 1)))

    return pl.pallas_call(
        weight_grad_kernel,
        grid=(4096 // TILE,),
        out_shape=jax.ShapeDtypeStruct((768, 4096), jnp.bfloat16),
        in_specs=[pl.BlockSpec((128, 2 * CAP, 384), lambda i: (0, 0, 0))]
        + [columns(part) for part in range(3)],
        out_specs=pl.BlockSpec((768, TILE), lambda i: (0, i)),
        scratch_shapes=[
            pltpu.VMEM((1536, 768), jnp.float32),
            pltpu.VMEM((768, 1536), jnp.bfloat16),
        ],
        compiler_params=pltpu.CompilerParams(vmem_limit_bytes=40 << 20),
        cost_estimate=pl.CostEstimate(
            flops=2 * 1536 * 768 * 4096, bytes_accessed=24 << 20, transcendentals=0
        ),
    )(got, *[rows.reshape(1536, width) for rows, width in zip(parts, WIDTHS)])


def restore_kernel(spot_ref, got_ref, out_ref, rows):
    def stage(block, carry):
        pieces = []
        for j in range(SIDE):
            piece = got_ref[block * SIDE + j].astype(jnp.float32)
            pieces.append(jnp.concatenate([piece[:CAP], piece[CAP:]], axis=1))
        first = pl.multiple_of(block * PICK, PICK)
        rows[pl.ds(first, PICK)] = jnp.concatenate(pieces, axis=0).astype(jnp.bfloat16)
        return carry

    lax.fori_loop(0, 32, stage, 0)
    for first in range(0, 1024, 256):
        place_of = lax.broadcasted_iota(jnp.int32, (256, 1536), 1)
        pick = jnp.where(spot_ref[first : first + 256] == place_of, 1.0, 0.0)
        out_ref[first : first + 256] = jnp.dot(
            pick.astype(jnp.bfloat16), rows[...], preferred_element_type=jnp.float32
        ).astype(jnp.bfloat16)


def restore(spot, got):
    vmem = pl.BlockSpec(memory_space=pltpu.VMEM)
    return pl.pallas_call(
        restore_kernel,
        out_shape=jax.ShapeDtypeStruct((1024, 768), jnp.bfloat16),
        in_specs=[vmem] * 2,
        out_specs=vmem,
        scratch_shapes=[pltpu.VMEM((1536, 768), jnp.bfloat16)],
        compiler_params=pltpu.CompilerParams(vmem_limit_bytes=24 << 20),
    )(spot, got)


def shards(hidden, out_grad, route_ids, gate_vals, rollout_ids, advantages, down_weight):
    slots = 1024
    named = jnp.sum(
        (route_ids[:, :, None] == jnp.arange(128, dtype=jnp.int32)).astype(jnp.bfloat16), axis=1
    )
    t = jnp.arange(128, dtype=jnp.int32)
    earlier = (t[:, None] > t[None, :]).astype(jnp.bfloat16)
    before = jnp.dot(earlier, named, preferred_element_type=jnp.float32)
    rank = jnp.sum(
        jnp.where(
            route_ids[:, :, None] == jnp.arange(128, dtype=jnp.int32), before[:, None, :], 0.0
        ),
        axis=2,
    ).astype(jnp.int32)
    spot = (route_ids * CAP + rank).reshape(slots)

    parts = dispatch(
        route_ids.T,
        gate_vals.T,
        rollout_ids,
        advantages,
        out_grad,
        spot[None, :],
        hidden.reshape(slots, 768),
        down_weight,
    )

    def exchange(rows):
        return lax.all_to_all(rows, ("grp", "ep"), split_axis=0, concat_axis=0, tiled=True)

    got_hidden = parts[4]
    returned = exchange(parts[3])
    weight_grad = weight_gradient(got_hidden, parts[:3])
    hidden_grad = restore(spot[:, None], returned)
    return hidden_grad.reshape(128, 8, 768), weight_grad[None]


def solution(mesh):
    wide = P(("grp", "ep"), None, None)
    flat = P(("grp", "ep"), None)
    return jax.shard_map(
        shards,
        mesh=mesh,
        in_specs=(wide, flat, flat, flat, flat, flat, wide),
        out_specs=(wide, wide),
        check_vma=False,
    )
```
